32 devices in a mesh: groups: 2 (over x), depth: 16 (over z, y, core).
Axes of the slice: x: 2, y: 2, z: 4, core: 2. Of those that a mesh axis runs over, the one named last changes fastest.
Arguments:
- fields: float32 [32, 2, 2, 512, 256], P(('groups', 'depth')), parts along dimension 0, may hold values from -6 to 6
- vel_tiles: float32 [64, 128, 128], P(('groups', 'depth')), parts along dimension 0, may hold values from 0.5 to 2
- tile_ids: int32 [32, 2, 4, 2], P(('groups', 'depth')), parts along dimension 0, may hold values from 0 to 31
- orders: int32 [32, 2], P(('groups', 'depth')), parts along dimension 0, may hold values from 1 to 3
- term_weights: float32 [3], replicated, may hold values from 0.05 to 0.12
- phase_rates: float32 [4], replicated, may hold values from 1 to 4
- owners: int32 [32, 16], P(('groups', 'depth')), parts along dimension 0, may hold values from 0 to 15, as said below
- image_slots: int32 [32, 16], P(('groups', 'depth')), parts along dimension 0, may hold values from 0 to 7
Outputs:
- image_volume: float32 [256, 128, 128], P(('groups', 'depth')), parts along dimension 0
- wavefields_out: float32 [32, 2, 2, 512, 256], P(('groups', 'depth')), parts along dimension 0
The draws below stay inside these ranges and needn't reach their ends.
There are 2 independent parts, one for each index of `groups`. The reference program is written for one: setup_inputs(seed, part) draws one part's arguments, and reference() takes and returns one part's arrays. A program takes and returns all parts, laid end to end along the dimension named above; an argument that names none is the same for every part. Nothing has to cross between parts.
Inputs may be any that keep to these rules, and one draw needn't show every extreme that they name: `owners`: of the 16 tiles of one slab, at most 2 have the same owner, and some owner gets exactly 2 of them.
All inputs are finite; a program needn't handle non-finite values.
Results may differ from the reference program's by a relative error of at most 0.0003.
Values sent between devices are 32-bit elements; how exact they have to be, the bound alone decides.
A program may use at most 64 MiB of HBM per device.

```python
import math
import jax
import jax.numpy as jnp

NX = 512
NY = 256
TS = 128
TICKS = 2
STEPS = 2
ORDER = 3
CAP = 2
IMG_SLOTS = 8
SECTIONS = 16
VTILES = 32
TX = 4
TY = 2
PIECES = 16


def draw_owners(key, part):

    def draw_slab(slab_index):
        slab_key = jax.random.fold_in(jax.random.fold_in(key, 7), slab_index)
        key_full, key_order, key_shuffle = jax.random.split(slab_key, 3)
        seat_total = SECTIONS * CAP
        full_owner = jax.random.randint(key_full, (), 0, SECTIONS)
        seat_rank = jnp.argsort(jax.random.permutation(key_order, seat_total))
        seats_all = jnp.arange(seat_total)
        scores = seat_rank + jnp.where(seats_all // CAP == full_owner, 0, seat_total)
        chosen = jnp.argsort(scores)[:PIECES]
        owner_list = (chosen // CAP).astype(jnp.int32)
        return owner_list[jax.random.permutation(key_shuffle, PIECES)]
    return jax.vmap(draw_slab)(jnp.arange(SECTIONS)).astype(jnp.int32)


def touch_ends(entries, key, smallest, top_value):
    index_at = [jax.random.randint(jax.random.fold_in(key, axis), (), 0, length) for axis, length in enumerate(entries.shape)]
    main_axis = entries.shape.index(max(entries.shape))
    next_to = index_at[:main_axis] + [(index_at[main_axis] + 1) % entries.shape[main_axis]] + index_at[main_axis + 1:]
    return entries.at[tuple(index_at)].set(smallest).at[tuple(next_to)].set(top_value)


def steps_of(own_key, dims, shards, low, largest):
    def one(axis_at, blocks):
        heights = jax.random.uniform(jax.random.fold_in(jax.random.fold_in(own_key, 6), axis_at), (blocks,), jnp.float32, low / len(shards), largest / len(shards))
        return jnp.repeat(jnp.exp(heights), dims[axis_at] // blocks).reshape((-1,) + (1,) * (len(dims) - axis_at - 1))

    factor_of = one(*shards[0])
    for cut in shards[1:]:
        factor_of = factor_of * one(*cut)
    return factor_of


def gaussian(own_key, shape, deviation, limit, shards=(), held_as=jnp.bfloat16):
    drawn = jax.random.normal(own_key, shape, jnp.float32) * deviation
    if len(shards) > 0:
        drawn = steps_of(own_key, shape, shards, -0.22, 0.18) * drawn
    return jnp.clip(drawn, min=-limit, max=limit).astype(held_as)


def setup_inputs(seed: int = 0, part: int = 0) -> dict:
    arg_keys = jax.random.split(jax.random.key(seed), 9)
    part_splits = jax.random.split(jax.random.fold_in(arg_keys[8], part), 9)
    return {
        "fields": gaussian(part_splits[0], (SECTIONS, 2, 2, NX, NY), 1.0, 6.0, ((0, 16),), jnp.float32),
        "vel_tiles": jnp.clip(jnp.exp(math.log(2.0) - 1.3862944 * jax.random.uniform(part_splits[1], (VTILES, TS, TS), jnp.float32) ** steps_of(part_splits[1], (VTILES, TS, TS), ((0, 16),), -0.2, 0.2)), 0.5, 2.0),
        "tile_ids": touch_ends(jax.random.randint(part_splits[2], (SECTIONS, STEPS, TX, TY), 0, VTILES), jax.random.fold_in(part_splits[2], 1), 0, VTILES - 1).astype(jnp.int32),
        "orders": touch_ends(jax.random.randint(part_splits[3], (SECTIONS, STEPS), 1, ORDER + 1), jax.random.fold_in(part_splits[3], 1), 1, ORDER).astype(jnp.int32),
        "term_weights": jnp.clip(jax.random.uniform(arg_keys[4], (ORDER,), jnp.float32, 0.05, 0.12), 0.05, 0.12),
        "phase_rates": jnp.clip(jax.random.uniform(arg_keys[5], (ORDER + 1,), jnp.float32, 1.0, 4.0), 1.0, 4.0),
        "owners": draw_owners(jax.random.fold_in(jax.random.fold_in(arg_keys[8], part), 71), part),
        "image_slots": touch_ends(jax.random.randint(part_splits[7], (SECTIONS, PIECES), 0, IMG_SLOTS), jax.random.fold_in(part_splits[7], 1), 0, IMG_SLOTS - 1).astype(jnp.int32),
    }


def mcclellan(fields_in):
    padded = jnp.pad(fields_in, ((0, 0), (1, 1), (1, 1)))
    beside = padded[:, 2:, 1:-1] + padded[:, :-2, 1:-1] + padded[:, 1:-1, 2:] + padded[:, 1:-1, :-2]
    corner = padded[:, 2:, 2:] + padded[:, :-2, :-2] + padded[:, 2:, :-2] + padded[:, :-2, 2:]
    return -0.5 * fields_in + 0.25 * beside + 0.125 * corner


def rotate_add(result, series_term, real_part, imag_part, pair_signs):
    pieces_out = []
    for pair_index, pair_sign in enumerate(pair_signs):
        real_in = series_term[2 * pair_index]
        imag_in = series_term[2 * pair_index + 1]
        pieces_out.append(result[2 * pair_index] + real_part * real_in - pair_sign * imag_part * imag_in)
        pieces_out.append(result[2 * pair_index + 1] + real_part * imag_in + pair_sign * imag_part * real_in)
    return jnp.stack(pieces_out)


def reference_step(wave_state, slowness_now, order_now, weights, phase_rates):
    result = jnp.zeros_like(wave_state)
    previous = wave_state
    current = wave_state
    for degree in range(ORDER + 1):
        if degree == 0:
            series_term = wave_state
        elif degree == 1:
            series_term = mcclellan(wave_state)
        else:
            series_term = 2.0 * mcclellan(current) - previous
        if degree >= 1:
            previous, current = current, series_term
        active = (degree <= order_now).astype(jnp.float32)
        angle_now = phase_rates[degree] * slowness_now
        real_part = weights[degree] * jnp.cos(angle_now) * active
        imag_part = weights[degree] * jnp.sin(angle_now) * active
        result = rotate_add(result, series_term, real_part, imag_part, (1.0, -1.0))
    return result


def reference(fields, vel_tiles, tile_ids, orders, term_weights, phase_rates, owners, image_slots):
    sections = fields.shape[0]
    cells_x = fields.shape[3]
    cells_y = fields.shape[4]
    picked = vel_tiles[tile_ids]
    slowness = picked.transpose(0, 1, 2, 4, 3, 5).reshape(sections, STEPS, cells_x, cells_y)
    weights = jnp.concatenate([(1.0 - jnp.sum(term_weights))[None], term_weights])
    wave_state = fields.reshape(sections, 4, cells_x, cells_y)
    image_sum = jnp.zeros((sections, STEPS, cells_x, cells_y), jnp.float32)
    stepper = jax.vmap(reference_step, in_axes=(0, 0, 0, None, None))
    for tick_index in range(TICKS):
        if tick_index > 0:
            wave_state = jnp.concatenate([jnp.zeros_like(wave_state[:1]), wave_state[:-1]], 0)
        for step_index in range(STEPS):
            wave_state = stepper(wave_state, slowness[:, step_index], orders[:, step_index], weights, phase_rates)
            product = wave_state[:, 0] * wave_state[:, 2] + wave_state[:, 1] * wave_state[:, 3]
            image_sum = image_sum.at[:, step_index].add(product)
    tile_rows = image_sum.reshape(sections, STEPS, TX, TS, TY, TS).transpose(0, 1, 2, 4, 3, 5)
    tile_rows = tile_rows.reshape(sections * PIECES, TS * TS)
    targets = (owners * IMG_SLOTS + image_slots).reshape(-1).astype(jnp.int32)
    volume = jax.ops.segment_sum(tile_rows, targets, num_segments=sections * IMG_SLOTS)
    return volume.reshape(sections * IMG_SLOTS, TS, TS), wave_state.reshape(fields.shape)
```

```python
import jax
import jax.numpy as jnp
from jax import lax
from jax.experimental import pallas as pl
from jax.experimental.pallas import tpu as pltpu
from jax.sharding import PartitionSpec as P

TICKS = 2
CAP = 2
IMG_SLOTS = 8
LANES = 128
HALO = 8
ROWS = 32
VMEM = pltpu.VMEM
SMEM = pltpu.SMEM


def specs(*spaces):
    return [pl.BlockSpec(memory_space=space) for space in spaces]


def from_behind(shard, axis, by):
    peers = lax.axis_size(axis)
    pairs = [(i, i + by) for i in range(peers) if 0 <= i + by < peers]
    return lax.ppermute(shard, axis, pairs)


def sincos(angle):
    turns = jnp.floor(angle * 0.6366197723675814 + 0.5)
    quarter = turns.astype(jnp.int32)
    r = angle - turns * 1.5703125
    r = r - turns * 4.837512969970703e-4
    r = r - turns * 7.54978995489188e-8
    r2 = r * r
    s = r + r * r2 * (-1.6666654611e-1 + r2 * (8.3321608736e-3 - r2 * 1.9515295891e-4))
    c = 1.0 - 0.5 * r2 + r2 * r2 * (
        4.166664568298827e-2 + r2 * (-1.388731625493765e-3 + r2 * 2.443315711809948e-5)
    )
    odd = (quarter & 1) == 1
    sin_out = jnp.where(odd, c, s)
    cos_out = jnp.where(odd, s, c)
    sin_out = jnp.where((quarter & 2) == 2, -sin_out, sin_out)
    cos_out = jnp.where(((quarter + 1) & 2) == 2, -cos_out, cos_out)
    return sin_out, cos_out


def table_kernel(ids_ref, orders_ref, term_ref, rates_ref, library_ref, table_ref):
    _, steps, tiles_x, tiles_y = ids_ref.shape
    degrees = rates_ref.shape[0]
    tile = library_ref.shape[1]
    zeroth = 1.0 - sum(term_ref[k] for k in range(degrees - 1))
    for j in range(steps):
        order = orders_ref[0, j]
        weights = [zeroth] + [
            jnp.where(order >= k, term_ref[k - 1], 0.0) for k in range(1, degrees)
        ]
        for b in range(tiles_y):
            for a in range(tiles_x):
                source = ids_ref[0, j, a, b]

                def body(i, _):
                    r0 = pl.multiple_of(i * ROWS, ROWS)
                    slow = library_ref[source, pl.ds(r0, ROWS), :]
                    for k in range(degrees):
                        sin_now, cos_now = sincos(rates_ref[k] * slow)
                        rows = pl.ds(a * tile + r0, ROWS)
                        table_ref[j, k, 0, b, rows, :] = weights[k] * cos_now
                        table_ref[j, k, 1, b, rows, :] = weights[k] * sin_now
                    return 0

                lax.fori_loop(0, tile // ROWS, body, 0)


def smooth(ref, f, halves, r0, lane):
    centre, down = [], []
    for h in range(halves):
        c = ref[f, h, pl.ds(r0 + HALO, ROWS), :]
        u = ref[f, h, pl.ds(r0 + HALO - 1, ROWS), :]
        d = ref[f, h, pl.ds(r0 + HALO + 1, ROWS), :]
        centre.append(c)
        down.append((u + d) + (c + c))
    right = [pltpu.roll(v, 1, 1) for v in down]
    left = [pltpu.roll(v, LANES - 1, 1) for v in down]
    out = []
    for h in range(halves):
        before = jnp.where(lane == 0, right[h - 1] if h else 0.0, right[h])
        after = jnp.where(lane == LANES - 1, left[h + 1] if h + 1 < halves else 0.0, left[h])
        out.append((before + after) + (down[h] + down[h]))
    return out, centre


def clear_halos(refs, halves, rows):
    zero = jnp.zeros((HALO, LANES), jnp.float32)
    for ref in refs:
        for f in range(2):
            for h in range(halves):
                ref[f, h, 0:HALO, :] = zero
                ref[f, h, rows + HALO : rows + 2 * HALO, :] = zero


def load_state(state_ref, p0, halves, rows):
    def body(i, _):
        r0 = pl.multiple_of(i * ROWS, ROWS)
        for f in range(2):
            for h in range(halves):
                p0[f, h, pl.ds(r0 + HALO, ROWS), :] = state_ref[
                    f, pl.ds(r0, ROWS), h * LANES : (h + 1) * LANES
                ]
        return 0

    lax.fori_loop(0, rows // ROWS, body, 0)


def depth_step(table_ref, j, sign, p0, p1, p2, halves, rows, emit):
    lane = lax.broadcasted_iota(jnp.int32, (ROWS, LANES), 1)
    chunks = rows // ROWS

    def first(i, _):
        r0 = pl.multiple_of(i * ROWS, ROWS)
        for f in range(2):
            soft, centre = smooth(p0, f, halves, r0, lane)
            for h in range(halves):
                p1[f, h, pl.ds(r0 + HALO, ROWS), :] = 0.125 * soft[h] - centre[h]
        return 0

    def second(i, _):
        r0 = pl.multiple_of(i * ROWS, ROWS)
        for f in range(2):
            soft, centre = smooth(p1, f, halves, r0, lane)
            for h in range(halves):
                here = pl.ds(r0 + HALO, ROWS)
                p2[f, h, here, :] = 0.25 * soft[h] - 2.0 * centre[h] - p0[f, h, here, :]
        return 0

    def third(i, _):
        r0 = pl.multiple_of(i * ROWS, ROWS)
        here = pl.ds(r0 + HALO, ROWS)
        terms = []
        for f in range(2):
            soft, centre = smooth(p2, f, halves, r0, lane)
            terms.append((soft, centre))
        for h in range(halves):
            series = []
            for f in range(2):
                soft, centre = terms[f]
                t0 = p0[f, h, here, :]
                t1 = p1[f, h, here, :]
                series.append((t0, t1, centre[h], 0.25 * soft[h] - 2.0 * centre[h] - t1))
            real = imag = None
            for k in range(4):
                a = table_ref[j, k, 0, h, pl.ds(r0, ROWS), :]
                b = table_ref[j, k, 1, h, pl.ds(r0, ROWS), :]
                re, im = series[0][k], series[1][k]
                if sign > 0:
                    new_real, new_imag = a * re - b * im, a * im + b * re
                else:
                    new_real, new_imag = a * re + b * im, a * im - b * re
                real = new_real if real is None else real + new_real
                imag = new_imag if imag is None else imag + new_imag
            p0[0, h, here, :] = real
            p0[1, h, here, :] = imag
            emit(j, h, r0, real, imag)
        return 0

    lax.fori_loop(0, chunks, first, 0)
    lax.fori_loop(0, chunks, second, 0)
    lax.fori_loop(0, chunks, third, 0)


def source_kernel(table_ref, state_ref, out_ref, p0, p1, p2):
    halves, rows = table_ref.shape[3], table_ref.shape[4]
    clear_halos((p0, p1, p2), halves, rows)
    load_state(state_ref, p0, halves, rows)

    def emit(j, h, r0, real, imag):
        columns = slice(h * LANES, (h + 1) * LANES)
        out_ref[j, 0, pl.ds(r0, ROWS), columns] = real
        out_ref[j, 1, pl.ds(r0, ROWS), columns] = imag

    for j in range(table_ref.shape[0]):
        depth_step(table_ref, j, 1.0, p0, p1, p2, halves, rows, emit)


def receiver_kernel(table_ref, state_ref, steps_ref, out_ref, corr_ref, p0, p1, p2):
    halves, rows = table_ref.shape[3], table_ref.shape[4]
    clear_halos((p0, p1, p2), halves, rows)
    load_state(state_ref, p0, halves, rows)
    last = table_ref.shape[0] - 1

    def emit(j, h, r0, real, imag):
        columns = slice(h * LANES, (h + 1) * LANES)
        here = pl.ds(r0, ROWS)
        if j == last:
            out_ref[0, here, columns] = real
            out_ref[1, here, columns] = imag
        corr_ref[j, h, here, :] = (
            steps_ref[j, 0, here, columns] * real + steps_ref[j, 1, here, columns] * imag
        )

    for j in range(last + 1):
        depth_step(table_ref, j, -1.0, p0, p1, p2, halves, rows, emit)


def final_kernel(
    owners_ref, slots_ref, table_ref, state_ref, steps_ref, before_ref,
    wave_ref, buffer_ref, corr, p0, p1, p2,
):
    halves, rows = table_ref.shape[3], table_ref.shape[4]
    clear_halos((p0, p1, p2), halves, rows)
    load_state(state_ref, p0, halves, rows)
    steps = table_ref.shape[0]
    last = steps - 1
    tile = LANES
    tiles_x = rows // tile

    def emit(j, h, r0, real, imag):
        columns = slice(h * LANES, (h + 1) * LANES)
        here = pl.ds(r0, ROWS)
        src_real = steps_ref[j, 0, here, columns]
        src_imag = steps_ref[j, 1, here, columns]
        if j == last:
            wave_ref[0, 0, 0, here, columns] = src_real
            wave_ref[0, 0, 1, here, columns] = src_imag
            wave_ref[0, 1, 0, here, columns] = real
            wave_ref[0, 1, 1, here, columns] = imag
        corr[j, h, here, :] = before_ref[j, h, here, :] + (src_real * real + src_imag * imag)

    for j in range(steps):
        depth_step(table_ref, j, -1.0, p0, p1, p2, halves, rows, emit)

    peers = buffer_ref.shape[0]

    def clear(o, _):
        buffer_ref[o] = jnp.zeros(buffer_ref.shape[1:], jnp.float32)
        buffer_ref[o, CAP * tile : CAP * tile + CAP, :] = jnp.full((CAP, LANES), -1.0, jnp.float32)
        return 0

    lax.fori_loop(0, peers, clear, 0)
    pieces = owners_ref.shape[1]

    for p in range(pieces):
        owner = owners_ref[0, p]
        rank = 0
        for q in range(p):
            rank = rank + jnp.where(owners_ref[0, q] == owner, 1, 0)
        j, rest = divmod(p, tiles_x * halves)
        a, h = divmod(rest, halves)
        buffer_ref[owner, pl.ds(pl.multiple_of(rank * tile, tile), tile), :] = corr[
            j, h, a * tile : (a + 1) * tile, :
        ]
        slot = slots_ref[0, p].astype(jnp.float32)
        buffer_ref[owner, pl.ds(CAP * tile + rank, 1), :] = jnp.full((1, LANES), slot, jnp.float32)


def volume_kernel(received_ref, volume_ref):
    peers = received_ref.shape[0]
    tile = volume_ref.shape[1]
    step = 16

    def body(i, _):
        r0 = pl.multiple_of(i * step, step)

        def add(peer, sums):
            sums = list(sums)
            for c in range(CAP):
                slot = received_ref[peer, CAP * tile + c : CAP * tile + c + 1, :]
                slot = jnp.broadcast_to(slot, (step, LANES))
                piece = received_ref[peer, pl.ds(c * tile + r0, step), :]
                for m in range(IMG_SLOTS):
                    sums[m] = sums[m] + jnp.where(slot == m, piece, 0.0)
            return tuple(sums)

        zero = jnp.zeros((step, LANES), jnp.float32)
        sums = lax.fori_loop(0, peers, add, (zero,) * IMG_SLOTS)
        for m in range(IMG_SLOTS):
            volume_ref[m, pl.ds(r0, step), :] = sums[m]
        return 0

    lax.fori_loop(0, tile // step, body, 0)


def local(fields, vel_tiles, tile_ids, orders, term_weights, phase_rates, owners, image_slots):
    rows, columns = fields.shape[3:]
    tile = vel_tiles.shape[1]
    steps = tile_ids.shape[1]
    degrees = phase_rates.shape[0]
    halves = columns // LANES
    peers = lax.axis_size("depth")
    f32 = jnp.float32

    def shape(*dims):
        return jax.ShapeDtypeStruct(dims, f32)

    cost = pl.CostEstimate(flops=40_000_000, bytes_accessed=14_000_000, transcendentals=0)
    padded = [VMEM((2, halves, rows + 2 * HALO, LANES), f32)] * 3

    library = lax.all_gather(vel_tiles, "depth", axis=0, tiled=True)
    table = pl.pallas_call(
        table_kernel,
        out_shape=shape(steps, degrees, 2, halves, rows, LANES),
        in_specs=specs(SMEM, SMEM, SMEM, SMEM, VMEM),
        out_specs=specs(VMEM)[0],
        name="table",
    )(tile_ids, orders, term_weights, phase_rates, library)

    source_call = pl.pallas_call(
        source_kernel,
        out_shape=shape(steps, 2, rows, columns),
        in_specs=specs(VMEM, VMEM),
        out_specs=specs(VMEM)[0],
        scratch_shapes=padded,
        cost_estimate=cost,
        name="source_step",
    )
    receiver_call = pl.pallas_call(
        receiver_kernel,
        out_shape=(shape(2, rows, columns), shape(steps, halves, rows, LANES)),
        in_specs=specs(VMEM, VMEM, VMEM),
        out_specs=specs(VMEM, VMEM),
        scratch_shapes=padded,
        cost_estimate=cost,
        name="receiver_step",
    )
    final_call = pl.pallas_call(
        final_kernel,
        out_shape=(
            shape(1, 2, 2, rows, columns),
            shape(peers, CAP * tile + HALO, LANES),
        ),
        in_specs=specs(SMEM, SMEM, VMEM, VMEM, VMEM, VMEM),
        out_specs=specs(VMEM, VMEM),
        scratch_shapes=[VMEM((steps, halves, rows, LANES), f32)] + padded,
        cost_estimate=cost,
        name="final_step",
    )

    source_steps = source_call(table, fields[0, 0])
    source = from_behind(source_steps[steps - 1], "depth", 1)
    receiver, correlation = receiver_call(table, fields[0, 1], source_steps)
    receiver = from_behind(receiver, "depth", 1)
    source_steps = source_call(table, source)
    wave, buffer = final_call(owners, image_slots, table, receiver, source_steps, correlation)
    received = lax.all_to_all(buffer, "depth", split_axis=0, concat_axis=0, tiled=True)
    volume = pl.pallas_call(
        volume_kernel,
        out_shape=shape(IMG_SLOTS, tile, LANES),
        in_specs=specs(VMEM),
        out_specs=specs(VMEM)[0],
        name="volume",
    )(received)
    return volume, wave


def solution(mesh):
    whole = P(("groups", "depth"))
    placed = (whole, whole, whole, whole, P(), P(), whole, whole)
    return jax.shard_map(
        local, mesh=mesh, in_specs=placed, out_specs=(whole, whole), check_vma=False
    )
```

```python
import jax
import jax.numpy as jnp
from jax import lax
from jax.experimental import pallas as pl
from jax.experimental.pallas import tpu as pltpu
from jax.sharding import PartitionSpec as P

TICKS = 2
CAP = 2
IMG_SLOTS = 8
LANES = 128
HALO = 8
ROWS = 32
VMEM = pltpu.VMEM
SMEM = pltpu.SMEM


def specs(*spaces):
    return [pl.BlockSpec(memory_space=space) for space in spaces]


def from_behind(shard, axis, by):
    peers = lax.axis_size(axis)
    pairs = [(i, i + by) for i in range(peers) if 0 <= i + by < peers]
    return lax.ppermute(shard, axis, pairs)


def sincos(angle):
    turns = jnp.floor(angle * 0.6366197723675814 + 0.5)
    quarter = turns.astype(jnp.int32)
    r = angle - turns * 1.5703125
    r = r - turns * 4.837512969970703e-4
    r = r - turns * 7.54978995489188e-8
    r2 = r * r
    s = r + r * r2 * (-1.6666654611e-1 + r2 * (8.3321608736e-3 - r2 * 1.9515295891e-4))
    c = 1.0 - 0.5 * r2 + r2 * r2 * (
        4.166664568298827e-2 + r2 * (-1.388731625493765e-3 + r2 * 2.443315711809948e-5)
    )
    odd = (quarter & 1) == 1
    sin_out = jnp.where(odd, c, s)
    cos_out = jnp.where(odd, s, c)
    sin_out = jnp.where((quarter & 2) == 2, -sin_out, sin_out)
    cos_out = jnp.where(((quarter + 1) & 2) == 2, -cos_out, cos_out)
    return sin_out, cos_out


def table_kernel(ids_ref, orders_ref, term_ref, rates_ref, library_ref, table_ref):
    _, steps, tiles_x, tiles_y = ids_ref.shape
    degrees = rates_ref.shape[0]
    tile = library_ref.shape[1]
    zeroth = 1.0 - sum(term_ref[k] for k in range(degrees - 1))
    for j in range(steps):
        order = orders_ref[0, j]
        weights = [zeroth] + [
            jnp.where(order >= k, term_ref[k - 1], 0.0) for k in range(1, degrees)
        ]
        for b in range(tiles_y):
            for a in range(tiles_x):
                source = ids_ref[0, j, a, b]

                def body(i, _):
                    r0 = pl.multiple_of(i * ROWS, ROWS)
                    slow = library_ref[source, pl.ds(r0, ROWS), :]
                    for k in range(degrees):
                        sin_now, cos_now = sincos(rates_ref[k] * slow)
                        rows = pl.ds(a * tile + r0, ROWS)
                        table_ref[j, k, 0, b, rows, :] = weights[k] * cos_now
                        table_ref[j, k, 1, b, rows, :] = weights[k] * sin_now
                    return 0

                lax.fori_loop(0, tile // ROWS, body, 0)


def smooth(ref, f, halves, r0, lane):
    centre, down = [], []
    for h in range(halves):
        c = ref[f, h, pl.ds(r0 + HALO, ROWS), :]
        u = ref[f, h, pl.ds(r0 + HALO - 1, ROWS), :]
        d = ref[f, h, pl.ds(r0 + HALO + 1, ROWS), :]
        centre.append(c)
        down.append((u + d) + (c + c))
    right = [pltpu.roll(v, 1, 1) for v in down]
    left = [pltpu.roll(v, LANES - 1, 1) for v in down]
    out = []
    for h in range(halves):
        before = jnp.where(lane == 0, right[h - 1] if h else 0.0, right[h])
        after = jnp.where(lane == LANES - 1, left[h + 1] if h + 1 < halves else 0.0, left[h])
        out.append((before + after) + (down[h] + down[h]))
    return out, centre


def clear_halos(refs, halves, rows):
    zero = jnp.zeros((HALO, LANES), jnp.float32)
    for ref in refs:
        for f in range(2):
            for h in range(halves):
                ref[f, h, 0:HALO, :] = zero
                ref[f, h, rows + HALO : rows + 2 * HALO, :] = zero


def load_state(state_ref, p0, halves, rows):
    def body(i, _):
        r0 = pl.multiple_of(i * ROWS, ROWS)
        for f in range(2):
            for h in range(halves):
                p0[f, h, pl.ds(r0 + HALO, ROWS), :] = state_ref[
                    f, pl.ds(r0, ROWS), h * LANES : (h + 1) * LANES
                ]
        return 0

    lax.fori_loop(0, rows // ROWS, body, 0)


def depth_step(table_ref, j, sign, p0, p1, p2, halves, rows, emit):
    lane = lax.broadcasted_iota(jnp.int32, (ROWS, LANES), 1)
    chunks = rows // ROWS

    def first(i, _):
        r0 = pl.multiple_of(i * ROWS, ROWS)
        for f in range(2):
            soft, centre = smooth(p0, f, halves, r0, lane)
            for h in range(halves):
                p1[f, h, pl.ds(r0 + HALO, ROWS), :] = 0.125 * soft[h] - centre[h]
        return 0

    def second(i, _):
        r0 = pl.multiple_of(i * ROWS, ROWS)
        for f in range(2):
            soft, centre = smooth(p1, f, halves, r0, lane)
            for h in range(halves):
                here = pl.ds(r0 + HALO, ROWS)
                p2[f, h, here, :] = 0.25 * soft[h] - 2.0 * centre[h] - p0[f, h, here, :]
        return 0

    def third(i, _):
        r0 = pl.multiple_of(i * ROWS, ROWS)
        here = pl.ds(r0 + HALO, ROWS)
        terms = []
        for f in range(2):
            soft, centre = smooth(p2, f, halves, r0, lane)
            terms.append((soft, centre))
        for h in range(halves):
            series = []
            for f in range(2):
                soft, centre = terms[f]
                t0 = p0[f, h, here, :]
                t1 = p1[f, h, here, :]
                series.append((t0, t1, centre[h], 0.25 * soft[h] - 2.0 * centre[h] - t1))
            real = imag = None
            for k in range(4):
                a = table_ref[j, k, 0, h, pl.ds(r0, ROWS), :]
                b = table_ref[j, k, 1, h, pl.ds(r0, ROWS), :]
                re, im = series[0][k], series[1][k]
                if sign > 0:
                    new_real, new_imag = a * re - b * im, a * im + b * re
                else:
                    new_real, new_imag = a * re + b * im, a * im - b * re
                real = new_real if real is None else real + new_real
                imag = new_imag if imag is None else imag + new_imag
            p0[0, h, here, :] = real
            p0[1, h, here, :] = imag
            emit(j, h, r0, real, imag)
        return 0

    lax.fori_loop(0, chunks, first, 0)
    lax.fori_loop(0, chunks, second, 0)
    lax.fori_loop(0, chunks, third, 0)


def source_kernel(table_ref, state_ref, out_ref, end_ref, p0, p1, p2):
    halves, rows = table_ref.shape[3], table_ref.shape[4]
    clear_halos((p0, p1, p2), halves, rows)
    load_state(state_ref, p0, halves, rows)

    def emit(j, h, r0, real, imag):
        columns = slice(h * LANES, (h + 1) * LANES)
        here = pl.ds(r0, ROWS)
        target = end_ref if j == table_ref.shape[0] - 1 else out_ref.at[j]
        target[0, here, columns] = real
        target[1, here, columns] = imag

    for j in range(table_ref.shape[0]):
        depth_step(table_ref, j, 1.0, p0, p1, p2, halves, rows, emit)


def receiver_kernel(table_ref, state_ref, steps_ref, end_ref, out_ref, corr_ref, p0, p1, p2):
    halves, rows = table_ref.shape[3], table_ref.shape[4]
    clear_halos((p0, p1, p2), halves, rows)
    load_state(state_ref, p0, halves, rows)
    last = table_ref.shape[0] - 1

    def emit(j, h, r0, real, imag):
        columns = slice(h * LANES, (h + 1) * LANES)
        here = pl.ds(r0, ROWS)
        if j == last:
            out_ref[0, here, columns] = real
            out_ref[1, here, columns] = imag
        source = end_ref if j == last else steps_ref.at[j]
        corr_ref[j, h, here, :] = source[0, here, columns] * real + source[1, here, columns] * imag

    for j in range(last + 1):
        depth_step(table_ref, j, -1.0, p0, p1, p2, halves, rows, emit)


def final_kernel(
    owners_ref, slots_ref, table_ref, state_ref, steps_ref, end_ref, before_ref,
    wave_ref, buffer_ref, corr, p0, p1, p2,
):
    halves, rows = table_ref.shape[3], table_ref.shape[4]
    clear_halos((p0, p1, p2), halves, rows)
    load_state(state_ref, p0, halves, rows)
    steps = table_ref.shape[0]
    last = steps - 1
    tile = LANES
    tiles_x = rows // tile

    def emit(j, h, r0, real, imag):
        columns = slice(h * LANES, (h + 1) * LANES)
        here = pl.ds(r0, ROWS)
        source = end_ref if j == last else steps_ref.at[j]
        src_real = source[0, here, columns]
        src_imag = source[1, here, columns]
        if j == last:
            wave_ref[0, 0, 0, here, columns] = src_real
            wave_ref[0, 0, 1, here, columns] = src_imag
            wave_ref[0, 1, 0, here, columns] = real
            wave_ref[0, 1, 1, here, columns] = imag
        corr[j, h, here, :] = before_ref[j, h, here, :] + (src_real * real + src_imag * imag)

    for j in range(steps):
        depth_step(table_ref, j, -1.0, p0, p1, p2, halves, rows, emit)

    peers = buffer_ref.shape[0]

    def clear(o, _):
        buffer_ref[o] = jnp.zeros(buffer_ref.shape[1:], jnp.float32)
        buffer_ref[o, CAP * tile : CAP * tile + CAP, :] = jnp.full((CAP, LANES), -1.0, jnp.float32)
        return 0

    lax.fori_loop(0, peers, clear, 0)
    pieces = owners_ref.shape[1]

    for p in range(pieces):
        owner = owners_ref[0, p]
        rank = 0
        for q in range(p):
            rank = rank + jnp.where(owners_ref[0, q] == owner, 1, 0)
        j, rest = divmod(p, tiles_x * halves)
        a, h = divmod(rest, halves)
        buffer_ref[owner, pl.ds(pl.multiple_of(rank * tile, tile), tile), :] = corr[
            j, h, a * tile : (a + 1) * tile, :
        ]
        slot = slots_ref[0, p].astype(jnp.float32)
        buffer_ref[owner, pl.ds(CAP * tile + rank, 1), :] = jnp.full((1, LANES), slot, jnp.float32)


def remote(src, dst, send_sem, recv_sem, peer):
    return pltpu.make_async_remote_copy(
        src_ref=src, dst_ref=dst, send_sem=send_sem, recv_sem=recv_sem,
        device_id={"depth": peer}, device_id_type=pl.DeviceIdType.MESH,
    )


def meet(peers):
    barrier = pltpu.get_barrier_semaphore()
    for peer in peers:
        pl.semaphore_signal(
            barrier, inc=1, device_id={"depth": peer}, device_id_type=pl.DeviceIdType.MESH
        )
    pl.semaphore_wait(barrier, len(peers))


def gather_kernel(own_ref, library_ref, send_sem, recv_sem):
    me = lax.axis_index("depth")
    planes = library_ref.shape[0] // 4
    within = me % 4
    plane = me // 4
    core = me % 2
    pair = (me // 2) % 2

    def at(steps):
        return ((plane + steps + planes) % planes) * 4 + within

    beside = plane * 4 + (1 - pair) * 2 + core
    twin = me + 1 - 2 * core
    above, below = at(1), at(-1)
    meet([above, below, beside, twin])
    sent = []

    def send(block, peer):
        src = own_ref if block is me else library_ref.at[block]
        n = len(sent)
        copy = remote(src, library_ref.at[block], send_sem.at[n], recv_sem.at[block], peer)
        copy.start()
        sent.append(copy)

    def arrive(block):
        remote(own_ref, library_ref.at[block], send_sem.at[0], recv_sem.at[block], twin).wait_recv()

    up = planes // 2
    down = planes - 1 - up
    if up > 0:
        send(me, above)
    if down > 0:
        send(me, below)
    send(me, beside)
    send(me, twin)
    library_ref[me] = own_ref[...]
    order = [0]
    for step in range(1, up + 1):
        block = at(-step)
        order.append(-step)
        arrive(block)
        if step < up:
            send(block, above)
        send(block, beside)
        send(block, twin)
        if step <= down:
            block = at(step)
            order.append(step)
            arrive(block)
            if step < down:
                send(block, below)
            send(block, beside)
            send(block, twin)
    shift = (1 - 2 * pair) * 2
    for step in order:
        block = at(step) + shift
        arrive(block)
        send(block, twin)
    flip = 1 - 2 * core
    for step in order:
        arrive(at(step) + flip)
        arrive(at(step) + shift + flip)
    for copy in sent:
        copy.wait_send()


def volume_kernel(buffer_ref, volume_ref, received, send_sem, recv_sem):
    me = lax.axis_index("depth")
    peers = buffer_ref.shape[0]
    tile = volume_ref.shape[1]
    step = 32
    meet([(me + d) % peers for d in range(1, peers)])
    copies = []
    for d in range(1, peers):
        to = (me + d) % peers
        copy = remote(buffer_ref.at[to], received.at[d], send_sem.at[d], recv_sem.at[d], to)
        copy.start()
        copies.append(copy)

    def clear(m, _):
        volume_ref[m] = jnp.zeros((tile, LANES), jnp.float32)
        return 0

    lax.fori_loop(0, volume_ref.shape[0], clear, 0)

    def add_from(ref, block):
        for c in range(CAP):
            slot = ref[block, CAP * tile + c : CAP * tile + c + 1, :]
            slot = jnp.broadcast_to(slot, (8, LANES))
            slot = jnp.concatenate([slot] * (step // 8), axis=0)

            def body(i, _):
                r0 = pl.multiple_of(i * step, step)
                piece = ref[block, pl.ds(c * tile + r0, step), :]
                for m in range(IMG_SLOTS):
                    here = pl.ds(r0, step)
                    volume_ref[m, here, :] += jnp.where(slot == m, piece, 0.0)
                return 0

            lax.fori_loop(0, tile // step, body, 0)

    add_from(buffer_ref, me)
    for d, copy in enumerate(copies, 1):
        copy.wait_recv()
        add_from(received, d)
    for copy in copies:
        copy.wait_send()


def local(fields, vel_tiles, tile_ids, orders, term_weights, phase_rates, owners, image_slots):
    rows, columns = fields.shape[3:]
    tile = vel_tiles.shape[1]
    steps = tile_ids.shape[1]
    degrees = phase_rates.shape[0]
    halves = columns // LANES
    peers = lax.axis_size("depth")
    f32 = jnp.float32

    def shape(*dims):
        return jax.ShapeDtypeStruct(dims, f32)

    cost = pl.CostEstimate(flops=40_000_000, bytes_accessed=14_000_000, transcendentals=0)
    padded = [VMEM((2, halves, rows + 2 * HALO, LANES), f32)] * 3

    library = pl.pallas_call(
        gather_kernel,
        out_shape=shape(peers, *vel_tiles.shape),
        in_specs=specs(VMEM),
        out_specs=specs(VMEM)[0],
        scratch_shapes=[pltpu.SemaphoreType.DMA((peers,)), pltpu.SemaphoreType.DMA((peers,))],
        compiler_params=pltpu.CompilerParams(collective_id=0, has_side_effects=True),
        name="gather",
    )(vel_tiles).reshape(peers * vel_tiles.shape[0], tile, tile)
    table = pl.pallas_call(
        table_kernel,
        out_shape=shape(steps, degrees, 2, halves, rows, LANES),
        in_specs=specs(SMEM, SMEM, SMEM, SMEM, VMEM),
        out_specs=specs(VMEM)[0],
        name="table",
    )(tile_ids, orders, term_weights, phase_rates, library)

    def half_of(which):
        return pl.BlockSpec(
            (None, None, 2, rows, columns), lambda i: (0, which, 0, 0, 0), memory_space=VMEM
        )

    def source_call(state, spec):
        return pl.pallas_call(
            source_kernel,
            grid=(1,),
            out_shape=(shape(max(steps - 1, 1), 2, rows, columns), shape(2, rows, columns)),
            in_specs=specs(VMEM) + [spec],
            out_specs=specs(VMEM, VMEM),
            scratch_shapes=padded,
            cost_estimate=cost,
            name="source_step",
        )(table, state)

    early, end = source_call(fields, half_of(0))
    source = from_behind(end, "depth", 1)
    receiver, correlation = pl.pallas_call(
        receiver_kernel,
        grid=(1,),
        out_shape=(shape(2, rows, columns), shape(steps, halves, rows, LANES)),
        in_specs=specs(VMEM) + [half_of(1)] + specs(VMEM, VMEM),
        out_specs=specs(VMEM, VMEM),
        scratch_shapes=padded,
        cost_estimate=cost,
        name="receiver_step",
    )(table, fields, early, end)
    receiver = from_behind(receiver, "depth", 1)
    early, end = source_call(source, specs(VMEM)[0])
    block_rows = CAP * tile + HALO
    wave, buffer = pl.pallas_call(
        final_kernel,
        out_shape=(shape(1, 2, 2, rows, columns), shape(peers, block_rows, LANES)),
        in_specs=specs(SMEM, SMEM, VMEM, VMEM, VMEM, VMEM, VMEM),
        out_specs=specs(VMEM, VMEM),
        scratch_shapes=[VMEM((steps, halves, rows, LANES), f32)] + padded,
        cost_estimate=cost,
        name="final_step",
    )(owners, image_slots, table, receiver, early, end, correlation)
    volume = pl.pallas_call(
        volume_kernel,
        out_shape=shape(IMG_SLOTS, tile, LANES),
        in_specs=specs(VMEM),
        out_specs=specs(VMEM)[0],
        scratch_shapes=[
            VMEM((peers, block_rows, LANES), f32),
            pltpu.SemaphoreType.DMA((peers,)),
            pltpu.SemaphoreType.DMA((peers,)),
        ],
        compiler_params=pltpu.CompilerParams(collective_id=1, has_side_effects=True),
        name="volume",
    )(buffer)
    return volume, wave


def solution(mesh):
    whole = P(("groups", "depth"))
    placed = (whole, whole, whole, whole, P(), P(), whole, whole)
    return jax.shard_map(
        local, mesh=mesh, in_specs=placed, out_specs=(whole, whole), check_vma=False
    )
```

```python
import jax
import jax.numpy as jnp
from jax import lax
from jax.experimental import pallas as pl
from jax.experimental.pallas import tpu as pltpu
from jax.sharding import PartitionSpec as P

TICKS = 2
CAP = 2
IMG_SLOTS = 8
LANES = 128
HALO = 8
ROWS = 32
VMEM = pltpu.VMEM
SMEM = pltpu.SMEM


def specs(*spaces):
    return [pl.BlockSpec(memory_space=space) for space in spaces]


def from_behind(shard, axis, by):
    peers = lax.axis_size(axis)
    pairs = [(i, i + by) for i in range(peers) if 0 <= i + by < peers]
    return lax.ppermute(shard, axis, pairs)


def sincos(angle):
    turns = jnp.floor(angle * 0.6366197723675814 + 0.5)
    quarter = turns.astype(jnp.int32)
    r = angle - turns * 1.5703125
    r = r - turns * 4.838267948966192e-4
    r2 = r * r
    s = r + r * r2 * (-1.6666654611e-1 + r2 * (8.3321608736e-3 - r2 * 1.9515295891e-4))
    c = 1.0 - 0.5 * r2 + r2 * r2 * (
        4.166664568298827e-2 + r2 * (-1.388731625493765e-3 + r2 * 2.443315711809948e-5)
    )
    odd = (quarter & 1) == 1
    sin_out = jnp.where(odd, c, s)
    cos_out = jnp.where(odd, s, c)
    sin_out = jnp.where((quarter & 2) == 2, -sin_out, sin_out)
    cos_out = jnp.where(((quarter + 1) & 2) == 2, -cos_out, cos_out)
    return sin_out, cos_out


def table_kernel(ids_ref, orders_ref, term_ref, rates_ref, library_ref, table_ref):
    _, steps, tiles_x, tiles_y = ids_ref.shape
    degrees = rates_ref.shape[0]
    tile = library_ref.shape[1]
    zeroth = 1.0 - sum(term_ref[k] for k in range(degrees - 1))
    for j in range(steps):
        order = orders_ref[0, j]
        weights = [zeroth] + [
            jnp.where(order >= k, term_ref[k - 1], 0.0) for k in range(1, degrees)
        ]
        for b in range(tiles_y):
            for a in range(tiles_x):
                source = ids_ref[0, j, a, b]

                def body(i, _):
                    r0 = pl.multiple_of(i * ROWS, ROWS)
                    slow = library_ref[source, pl.ds(r0, ROWS), :]
                    for k in range(degrees):
                        sin_now, cos_now = sincos(rates_ref[k] * slow)
                        rows = pl.ds(a * tile + r0, ROWS)
                        table_ref[j, k, 0, b, rows, :] = weights[k] * cos_now
                        table_ref[j, k, 1, b, rows, :] = weights[k] * sin_now
                    return 0

                lax.fori_loop(0, tile // ROWS, body, 0)


def smooth(ref, f, halves, r0, lane):
    centre, down = [], []
    for h in range(halves):
        c = ref[f, h, pl.ds(r0 + HALO, ROWS), :]
        u = ref[f, h, pl.ds(r0 + HALO - 1, ROWS), :]
        d = ref[f, h, pl.ds(r0 + HALO + 1, ROWS), :]
        centre.append(c)
        down.append((u + d) + (c + c))
    right = [pltpu.roll(v, 1, 1) for v in down]
    left = [pltpu.roll(v, LANES - 1, 1) for v in down]
    out = []
    for h in range(halves):
        before = jnp.where(lane == 0, right[h - 1] if h else 0.0, right[h])
        after = jnp.where(lane == LANES - 1, left[h + 1] if h + 1 < halves else 0.0, left[h])
        out.append((before + after) + (down[h] + down[h]))
    return out, centre


def clear_halos(refs, halves, rows):
    zero = jnp.zeros((HALO, LANES), jnp.float32)
    for ref in refs:
        for f in range(2):
            for h in range(halves):
                ref[f, h, 0:HALO, :] = zero
                ref[f, h, rows + HALO : rows + 2 * HALO, :] = zero


def load_state(state_ref, p0, halves, rows):
    def body(i, _):
        r0 = pl.multiple_of(i * ROWS, ROWS)
        for f in range(2):
            for h in range(halves):
                p0[f, h, pl.ds(r0 + HALO, ROWS), :] = state_ref[
                    f, pl.ds(r0, ROWS), h * LANES : (h + 1) * LANES
                ]
        return 0

    lax.fori_loop(0, rows // ROWS, body, 0)


def fetch(table_ref, table, sems):
    copies = [
        pltpu.make_async_copy(table_ref.at[j], table.at[j], sems.at[j])
        for j in range(table_ref.shape[0])
    ]
    for copy in copies:
        copy.start()
    return copies


def depth_step(table_ref, copy, j, sign, p0, p1, p2, halves, rows, emit):
    lane = lax.broadcasted_iota(jnp.int32, (ROWS, LANES), 1)
    chunks = rows // ROWS

    def first(i, _):
        r0 = pl.multiple_of(i * ROWS, ROWS)
        for f in range(2):
            soft, centre = smooth(p0, f, halves, r0, lane)
            for h in range(halves):
                p1[f, h, pl.ds(r0 + HALO, ROWS), :] = 0.125 * soft[h] - centre[h]
        return 0

    def second(i, _):
        r0 = pl.multiple_of(i * ROWS, ROWS)
        for f in range(2):
            soft, centre = smooth(p1, f, halves, r0, lane)
            for h in range(halves):
                here = pl.ds(r0 + HALO, ROWS)
                p2[f, h, here, :] = 0.25 * soft[h] - 2.0 * centre[h] - p0[f, h, here, :]
        return 0

    def third(i, _):
        r0 = pl.multiple_of(i * ROWS, ROWS)
        here = pl.ds(r0 + HALO, ROWS)
        terms = []
        for f in range(2):
            soft, centre = smooth(p2, f, halves, r0, lane)
            terms.append((soft, centre))
        for h in range(halves):
            series = []
            for f in range(2):
                soft, centre = terms[f]
                t0 = p0[f, h, here, :]
                t1 = p1[f, h, here, :]
                series.append((t0, t1, centre[h], 0.25 * soft[h] - 2.0 * centre[h] - t1))
            real = imag = None
            for k in range(4):
                a = table_ref[j, k, 0, h, pl.ds(r0, ROWS), :]
                b = table_ref[j, k, 1, h, pl.ds(r0, ROWS), :]
                re, im = series[0][k], series[1][k]
                if sign > 0:
                    new_real, new_imag = a * re - b * im, a * im + b * re
                else:
                    new_real, new_imag = a * re + b * im, a * im - b * re
                real = new_real if real is None else real + new_real
                imag = new_imag if imag is None else imag + new_imag
            p0[0, h, here, :] = real
            p0[1, h, here, :] = imag
            emit(j, h, r0, real, imag)
        return 0

    lax.fori_loop(0, chunks, first, 0, unroll=2)
    lax.fori_loop(0, chunks, second, 0, unroll=2)
    copy.wait()
    lax.fori_loop(0, chunks, third, 0)


def source_kernel(table_ref, state_ref, out_ref, end_ref, p0, p1, p2, table, sems):
    copies = fetch(table_ref, table, sems)
    halves, rows = table_ref.shape[3], table_ref.shape[4]
    clear_halos((p0, p1, p2), halves, rows)
    load_state(state_ref, p0, halves, rows)

    def emit(j, h, r0, real, imag):
        columns = slice(h * LANES, (h + 1) * LANES)
        here = pl.ds(r0, ROWS)
        target = end_ref if j == table_ref.shape[0] - 1 else out_ref.at[j]
        target[0, here, columns] = real
        target[1, here, columns] = imag

    for j in range(table_ref.shape[0]):
        depth_step(table, copies[j], j, 1.0, p0, p1, p2, halves, rows, emit)


def receiver_kernel(table_ref, state_ref, steps_ref, end_ref, out_ref, corr_ref, p0, p1, p2, table, sems):
    copies = fetch(table_ref, table, sems)
    halves, rows = table_ref.shape[3], table_ref.shape[4]
    clear_halos((p0, p1, p2), halves, rows)
    load_state(state_ref, p0, halves, rows)
    last = table_ref.shape[0] - 1

    def emit(j, h, r0, real, imag):
        columns = slice(h * LANES, (h + 1) * LANES)
        here = pl.ds(r0, ROWS)
        if j == last:
            out_ref[0, here, columns] = real
            out_ref[1, here, columns] = imag
        source = end_ref if j == last else steps_ref.at[j]
        corr_ref[j, h, here, :] = source[0, here, columns] * real + source[1, here, columns] * imag

    for j in range(last + 1):
        depth_step(table, copies[j], j, -1.0, p0, p1, p2, halves, rows, emit)


def final_kernel(
    owners_ref, slots_ref, table_ref, state_ref, steps_ref, end_ref, before_ref,
    wave_ref, buffer_ref, corr, p0, p1, p2, table, sems,
):
    copies = fetch(table_ref, table, sems)
    halves, rows = table_ref.shape[3], table_ref.shape[4]
    clear_halos((p0, p1, p2), halves, rows)
    load_state(state_ref, p0, halves, rows)
    steps = table_ref.shape[0]
    last = steps - 1
    tile = LANES
    tiles_x = rows // tile

    def emit(j, h, r0, real, imag):
        columns = slice(h * LANES, (h + 1) * LANES)
        here = pl.ds(r0, ROWS)
        source = end_ref if j == last else steps_ref.at[j]
        src_real = source[0, here, columns]
        src_imag = source[1, here, columns]
        if j == last:
            wave_ref[0, 0, 0, here, columns] = src_real
            wave_ref[0, 0, 1, here, columns] = src_imag
            wave_ref[0, 1, 0, here, columns] = real
            wave_ref[0, 1, 1, here, columns] = imag
        corr[j, h, here, :] = before_ref[j, h, here, :] + (src_real * real + src_imag * imag)

    for j in range(steps):
        depth_step(table, copies[j], j, -1.0, p0, p1, p2, halves, rows, emit)

    peers = buffer_ref.shape[0]

    def clear(o, _):
        buffer_ref[o] = jnp.zeros(buffer_ref.shape[1:], jnp.float32)
        buffer_ref[o, CAP * tile : CAP * tile + CAP, :] = jnp.full((CAP, LANES), -1.0, jnp.float32)
        return 0

    lax.fori_loop(0, peers, clear, 0)
    pieces = owners_ref.shape[1]

    for p in range(pieces):
        owner = owners_ref[0, p]
        rank = 0
        for q in range(p):
            rank = rank + jnp.where(owners_ref[0, q] == owner, 1, 0)
        j, rest = divmod(p, tiles_x * halves)
        a, h = divmod(rest, halves)
        buffer_ref[owner, pl.ds(pl.multiple_of(rank * tile, tile), tile), :] = corr[
            j, h, a * tile : (a + 1) * tile, :
        ]
        slot = slots_ref[0, p].astype(jnp.float32)
        buffer_ref[owner, pl.ds(CAP * tile + rank, 1), :] = jnp.full((1, LANES), slot, jnp.float32)


def remote(src, dst, send_sem, recv_sem, peer):
    return pltpu.make_async_remote_copy(
        src_ref=src, dst_ref=dst, send_sem=send_sem, recv_sem=recv_sem,
        device_id={"depth": peer}, device_id_type=pl.DeviceIdType.MESH,
    )


def meet(peers):
    barrier = pltpu.get_barrier_semaphore()
    for peer in peers:
        pl.semaphore_signal(
            barrier, inc=1, device_id={"depth": peer}, device_id_type=pl.DeviceIdType.MESH
        )
    pl.semaphore_wait(barrier, len(peers))


def gather_kernel(own_ref, library_ref, send_sem, recv_sem):
    me = lax.axis_index("depth")
    planes = library_ref.shape[0] // 4
    within = me % 4
    plane = me // 4
    core = me % 2
    pair = (me // 2) % 2

    def at(steps):
        return ((plane + steps + planes) % planes) * 4 + within

    beside = plane * 4 + (1 - pair) * 2 + core
    twin = me + 1 - 2 * core
    above, below = at(1), at(-1)
    meet([above, below, beside, twin])
    sent = []

    def send(block, peer):
        src = own_ref if block is me else library_ref.at[block]
        n = len(sent)
        copy = remote(src, library_ref.at[block], send_sem.at[n], recv_sem.at[block], peer)
        copy.start()
        sent.append(copy)

    def arrive(block):
        remote(own_ref, library_ref.at[block], send_sem.at[0], recv_sem.at[block], twin).wait_recv()

    up = planes // 2
    down = planes - 1 - up
    if up > 0:
        send(me, above)
    if down > 0:
        send(me, below)
    send(me, beside)
    send(me, twin)
    library_ref[me] = own_ref[...]
    order = [0]
    for step in range(1, up + 1):
        block = at(-step)
        order.append(-step)
        arrive(block)
        if step < up:
            send(block, above)
        send(block, beside)
        send(block, twin)
        if step <= down:
            block = at(step)
            order.append(step)
            arrive(block)
            if step < down:
                send(block, below)
            send(block, beside)
            send(block, twin)
    shift = (1 - 2 * pair) * 2
    for step in order:
        block = at(step) + shift
        arrive(block)
        send(block, twin)
    flip = 1 - 2 * core
    for step in order:
        arrive(at(step) + flip)
        arrive(at(step) + shift + flip)
    for copy in sent:
        copy.wait_send()


def volume_kernel(buffer_ref, volume_ref, received, send_sem, recv_sem):
    me = lax.axis_index("depth")
    peers = buffer_ref.shape[0]
    tile = volume_ref.shape[1]
    step = 32
    meet([(me + d) % peers for d in range(1, peers)])
    copies = []
    for d in range(1, peers):
        to = (me + d) % peers
        copy = remote(buffer_ref.at[to], received.at[d], send_sem.at[d], recv_sem.at[d], to)
        copy.start()
        copies.append(copy)

    def clear(m, _):
        volume_ref[m] = jnp.zeros((tile, LANES), jnp.float32)
        return 0

    lax.fori_loop(0, volume_ref.shape[0], clear, 0)

    def add_from(ref, block):
        for c in range(CAP):
            slot = ref[block, CAP * tile + c : CAP * tile + c + 1, :]
            slot = jnp.broadcast_to(slot, (8, LANES))
            slot = jnp.concatenate([slot] * (step // 8), axis=0)

            def body(i, _):
                r0 = pl.multiple_of(i * step, step)
                piece = ref[block, pl.ds(c * tile + r0, step), :]
                for m in range(IMG_SLOTS):
                    here = pl.ds(r0, step)
                    volume_ref[m, here, :] += jnp.where(slot == m, piece, 0.0)
                return 0

            lax.fori_loop(0, tile // step, body, 0)

    add_from(buffer_ref, me)
    for d, copy in enumerate(copies, 1):
        copy.wait_recv()
        add_from(received, d)
    for copy in copies:
        copy.wait_send()


def local(fields, vel_tiles, tile_ids, orders, term_weights, phase_rates, owners, image_slots):
    rows, columns = fields.shape[3:]
    tile = vel_tiles.shape[1]
    steps = tile_ids.shape[1]
    degrees = phase_rates.shape[0]
    halves = columns // LANES
    peers = lax.axis_size("depth")
    f32 = jnp.float32

    def shape(*dims):
        return jax.ShapeDtypeStruct(dims, f32)

    cost = pl.CostEstimate(flops=40_000_000, bytes_accessed=14_000_000, transcendentals=0)
    padded = [VMEM((2, halves, rows + 2 * HALO, LANES), f32)] * 3 + [
        VMEM((steps, degrees, 2, halves, rows, LANES), f32),
        pltpu.SemaphoreType.DMA((steps,)),
    ]

    library = pl.pallas_call(
        gather_kernel,
        out_shape=shape(peers, *vel_tiles.shape),
        in_specs=specs(VMEM),
        out_specs=specs(VMEM)[0],
        scratch_shapes=[pltpu.SemaphoreType.DMA((peers,)), pltpu.SemaphoreType.DMA((peers,))],
        compiler_params=pltpu.CompilerParams(collective_id=0, has_side_effects=True),
        name="gather",
    )(vel_tiles).reshape(peers * vel_tiles.shape[0], tile, tile)
    table = pl.pallas_call(
        table_kernel,
        out_shape=shape(steps, degrees, 2, halves, rows, LANES),
        in_specs=specs(SMEM, SMEM, SMEM, SMEM, VMEM),
        out_specs=specs(VMEM)[0],
        name="table",
    )(tile_ids, orders, term_weights, phase_rates, library)

    def half_of(which):
        return pl.BlockSpec(
            (None, None, 2, rows, columns), lambda i: (0, which, 0, 0, 0), memory_space=VMEM
        )

    def source_call(state, spec):
        return pl.pallas_call(
            source_kernel,
            grid=(1,),
            out_shape=(shape(max(steps - 1, 1), 2, rows, columns), shape(2, rows, columns)),
            in_specs=specs(pl.ANY) + [spec],
            out_specs=specs(VMEM, VMEM),
            scratch_shapes=padded,
            cost_estimate=cost,
            name="source_step",
        )(table, state)

    early, end = source_call(fields, half_of(0))
    source = from_behind(end, "depth", 1)
    receiver, correlation = pl.pallas_call(
        receiver_kernel,
        grid=(1,),
        out_shape=(shape(2, rows, columns), shape(steps, halves, rows, LANES)),
        in_specs=specs(pl.ANY) + [half_of(1)] + specs(VMEM, VMEM),
        out_specs=specs(VMEM, VMEM),
        scratch_shapes=padded,
        cost_estimate=cost,
        name="receiver_step",
    )(table, fields, early, end)
    receiver = from_behind(receiver, "depth", 1)
    early, end = source_call(source, specs(VMEM)[0])
    block_rows = CAP * tile + HALO
    wave, buffer = pl.pallas_call(
        final_kernel,
        out_shape=(shape(1, 2, 2, rows, columns), shape(peers, block_rows, LANES)),
        in_specs=specs(SMEM, SMEM, pl.ANY, VMEM, VMEM, VMEM, VMEM),
        out_specs=specs(VMEM, VMEM),
        scratch_shapes=[VMEM((steps, halves, rows, LANES), f32)] + padded,
        cost_estimate=cost,
        name="final_step",
    )(owners, image_slots, table, receiver, early, end, correlation)
    volume = pl.pallas_call(
        volume_kernel,
        out_shape=shape(IMG_SLOTS, tile, LANES),
        in_specs=specs(VMEM),
        out_specs=specs(VMEM)[0],
        scratch_shapes=[
            VMEM((peers, block_rows, LANES), f32),
            pltpu.SemaphoreType.DMA((peers,)),
            pltpu.SemaphoreType.DMA((peers,)),
        ],
        compiler_params=pltpu.CompilerParams(collective_id=1, has_side_effects=True),
        name="volume",
    )(buffer)
    return volume, wave


def solution(mesh):
    whole = P(("groups", "depth"))
    placed = (whole, whole, whole, whole, P(), P(), whole, whole)
    return jax.shard_map(
        local, mesh=mesh, in_specs=placed, out_specs=(whole, whole), check_vma=False
    )
```

```python
import jax
import jax.numpy as jnp
from jax import lax
from jax.experimental import pallas as pl
from jax.experimental.pallas import tpu as pltpu
from jax.sharding import PartitionSpec as P

TICKS = 2
CAP = 2
IMG_SLOTS = 8
LANES = 128
HALO = 8
ROWS = 32
VMEM = pltpu.VMEM
SMEM = pltpu.SMEM


def specs(*spaces):
    return [pl.BlockSpec(memory_space=space) for space in spaces]


def from_behind(shard, axis, by):
    peers = lax.axis_size(axis)
    pairs = [(i, i + by) for i in range(peers) if 0 <= i + by < peers]
    return lax.ppermute(shard, axis, pairs)


def sincos(angle):
    turns = jnp.floor(angle * 0.6366197723675814 + 0.5)
    quarter = turns.astype(jnp.int32)
    r = angle - turns * 1.5703125
    r = r - turns * 4.838267948966192e-4
    r2 = r * r
    s = r + r * r2 * (-1.6666654611e-1 + r2 * (8.3321608736e-3 - r2 * 1.9515295891e-4))
    c = 1.0 - 0.5 * r2 + r2 * r2 * (
        4.166664568298827e-2 + r2 * (-1.388731625493765e-3 + r2 * 2.443315711809948e-5)
    )
    odd = (quarter & 1) == 1
    sin_out = jnp.where(odd, c, s)
    cos_out = jnp.where(odd, s, c)
    sin_out = jnp.where((quarter & 2) == 2, -sin_out, sin_out)
    cos_out = jnp.where(((quarter + 1) & 2) == 2, -cos_out, cos_out)
    return sin_out, cos_out


def table_kernel(ids_ref, orders_ref, term_ref, rates_ref, library_ref, table_ref):
    _, steps, tiles_x, tiles_y = ids_ref.shape
    degrees = rates_ref.shape[0]
    tile = library_ref.shape[1]
    zeroth = 1.0 - sum(term_ref[k] for k in range(degrees - 1))
    for j in range(steps):
        order = orders_ref[0, j]
        weights = [zeroth] + [
            jnp.where(order >= k, term_ref[k - 1], 0.0) for k in range(1, degrees)
        ]
        for b in range(tiles_y):
            for a in range(tiles_x):
                source = ids_ref[0, j, a, b]

                def body(i, _):
                    r0 = pl.multiple_of(i * ROWS, ROWS)
                    slow = library_ref[source, pl.ds(r0, ROWS), :]
                    for k in range(degrees):
                        sin_now, cos_now = sincos(rates_ref[k] * slow)
                        rows = pl.ds(a * tile + r0, ROWS)
                        table_ref[j, k, 0, b, rows, :] = weights[k] * cos_now
                        table_ref[j, k, 1, b, rows, :] = weights[k] * sin_now
                    return 0

                lax.fori_loop(0, tile // ROWS, body, 0)


def smooth(ref, f, halves, r0, lane):
    centre, down = [], []
    for h in range(halves):
        c = ref[f, h, pl.ds(r0 + HALO, ROWS), :]
        u = ref[f, h, pl.ds(r0 + HALO - 1, ROWS), :]
        d = ref[f, h, pl.ds(r0 + HALO + 1, ROWS), :]
        centre.append(c)
        down.append((u + d) + (c + c))
    right = [pltpu.roll(v, 1, 1) for v in down]
    left = [pltpu.roll(v, LANES - 1, 1) for v in down]
    out = []
    for h in range(halves):
        before = jnp.where(lane == 0, right[h - 1] if h else 0.0, right[h])
        after = jnp.where(lane == LANES - 1, left[h + 1] if h + 1 < halves else 0.0, left[h])
        out.append((before + after) + (down[h] + down[h]))
    return out, centre


def clear_halos(refs, halves, rows):
    zero = jnp.zeros((HALO, LANES), jnp.float32)
    for ref in refs:
        for f in range(2):
            for h in range(halves):
                ref[f, h, 0:HALO, :] = zero
                ref[f, h, rows + HALO : rows + 2 * HALO, :] = zero


def load_state(state_ref, p0, halves, rows):
    def body(i, _):
        r0 = pl.multiple_of(i * ROWS, ROWS)
        for f in range(2):
            for h in range(halves):
                p0[f, h, pl.ds(r0 + HALO, ROWS), :] = state_ref[
                    f, pl.ds(r0, ROWS), h * LANES : (h + 1) * LANES
                ]
        return 0

    lax.fori_loop(0, rows // ROWS, body, 0)


def fetch(table_ref, table, sems):
    copies = [
        pltpu.make_async_copy(table_ref.at[j], table.at[j], sems.at[j])
        for j in range(table_ref.shape[0])
    ]
    for copy in copies:
        copy.start()
    return copies


def depth_step(table_ref, copy, j, sign, p0, p1, p2, halves, rows, emit):
    lane = lax.broadcasted_iota(jnp.int32, (ROWS, LANES), 1)
    chunks = rows // ROWS

    def first(i, _):
        r0 = pl.multiple_of(i * ROWS, ROWS)
        for f in range(2):
            soft, centre = smooth(p0, f, halves, r0, lane)
            for h in range(halves):
                p1[f, h, pl.ds(r0 + HALO, ROWS), :] = 0.125 * soft[h] - centre[h]
        return 0

    def second(i, _):
        r0 = pl.multiple_of(i * ROWS, ROWS)
        for f in range(2):
            soft, centre = smooth(p1, f, halves, r0, lane)
            for h in range(halves):
                here = pl.ds(r0 + HALO, ROWS)
                p2[f, h, here, :] = 0.25 * soft[h] - 2.0 * centre[h] - p0[f, h, here, :]
        return 0

    def third(i, _):
        r0 = pl.multiple_of(i * ROWS, ROWS)
        here = pl.ds(r0 + HALO, ROWS)
        terms = []
        for f in range(2):
            soft, centre = smooth(p2, f, halves, r0, lane)
            terms.append((soft, centre))
        for h in range(halves):
            series = []
            for f in range(2):
                soft, centre = terms[f]
                t0 = p0[f, h, here, :]
                t1 = p1[f, h, here, :]
                series.append((t0, t1, centre[h], 0.25 * soft[h] - 2.0 * centre[h] - t1))
            real = imag = None
            for k in range(4):
                a = table_ref[j, k, 0, h, pl.ds(r0, ROWS), :]
                b = table_ref[j, k, 1, h, pl.ds(r0, ROWS), :]
                re, im = series[0][k], series[1][k]
                if sign > 0:
                    new_real, new_imag = a * re - b * im, a * im + b * re
                else:
                    new_real, new_imag = a * re + b * im, a * im - b * re
                real = new_real if real is None else real + new_real
                imag = new_imag if imag is None else imag + new_imag
            p0[0, h, here, :] = real
            p0[1, h, here, :] = imag
            emit(j, h, r0, real, imag)
        return 0

    lax.fori_loop(0, chunks, first, 0, unroll=2)
    lax.fori_loop(0, chunks, second, 0, unroll=2)
    copy.wait()
    lax.fori_loop(0, chunks, third, 0)


def source_kernel(table_ref, state_ref, out_ref, end_ref, p0, p1, p2, table, sems):
    copies = fetch(table_ref, table, sems)
    halves, rows = table_ref.shape[3], table_ref.shape[4]
    clear_halos((p0, p1, p2), halves, rows)
    load_state(state_ref, p0, halves, rows)

    def emit(j, h, r0, real, imag):
        columns = slice(h * LANES, (h + 1) * LANES)
        here = pl.ds(r0, ROWS)
        target = end_ref if j == table_ref.shape[0] - 1 else out_ref.at[j]
        target[0, here, columns] = real
        target[1, here, columns] = imag

    for j in range(table_ref.shape[0]):
        depth_step(table, copies[j], j, 1.0, p0, p1, p2, halves, rows, emit)


def receiver_kernel(table_ref, state_ref, steps_ref, end_ref, out_ref, corr_ref, p0, p1, p2, table, sems):
    copies = fetch(table_ref, table, sems)
    halves, rows = table_ref.shape[3], table_ref.shape[4]
    clear_halos((p0, p1, p2), halves, rows)
    load_state(state_ref, p0, halves, rows)
    last = table_ref.shape[0] - 1

    def emit(j, h, r0, real, imag):
        columns = slice(h * LANES, (h + 1) * LANES)
        here = pl.ds(r0, ROWS)
        if j == last:
            out_ref[0, here, columns] = real
            out_ref[1, here, columns] = imag
        source = end_ref if j == last else steps_ref.at[j]
        corr_ref[j, h, here, :] = source[0, here, columns] * real + source[1, here, columns] * imag

    for j in range(last + 1):
        depth_step(table, copies[j], j, -1.0, p0, p1, p2, halves, rows, emit)


def final_kernel(
    owners_ref, slots_ref, table_ref, state_ref, steps_ref, end_ref, before_ref,
    wave_ref, buffer_ref, corr, p0, p1, p2, table, sems,
):
    copies = fetch(table_ref, table, sems)
    halves, rows = table_ref.shape[3], table_ref.shape[4]
    clear_halos((p0, p1, p2), halves, rows)
    load_state(state_ref, p0, halves, rows)
    steps = table_ref.shape[0]
    last = steps - 1
    tile = LANES
    tiles_x = rows // tile

    def emit(j, h, r0, real, imag):
        columns = slice(h * LANES, (h + 1) * LANES)
        here = pl.ds(r0, ROWS)
        source = end_ref if j == last else steps_ref.at[j]
        src_real = source[0, here, columns]
        src_imag = source[1, here, columns]
        if j == last:
            wave_ref[0, 0, 0, here, columns] = src_real
            wave_ref[0, 0, 1, here, columns] = src_imag
            wave_ref[0, 1, 0, here, columns] = real
            wave_ref[0, 1, 1, here, columns] = imag
        corr[j, h, here, :] = before_ref[j, h, here, :] + (src_real * real + src_imag * imag)

    for j in range(steps):
        depth_step(table, copies[j], j, -1.0, p0, p1, p2, halves, rows, emit)

    peers = buffer_ref.shape[0]

    def clear(o, _):
        buffer_ref[o] = jnp.zeros(buffer_ref.shape[1:], jnp.float32)
        buffer_ref[o, CAP * tile : CAP * tile + CAP, :] = jnp.full((CAP, LANES), -1.0, jnp.float32)
        return 0

    lax.fori_loop(0, peers, clear, 0)
    pieces = owners_ref.shape[1]

    for p in range(pieces):
        owner = owners_ref[0, p]
        rank = 0
        for q in range(p):
            rank = rank + jnp.where(owners_ref[0, q] == owner, 1, 0)
        j, rest = divmod(p, tiles_x * halves)
        a, h = divmod(rest, halves)
        buffer_ref[owner, pl.ds(pl.multiple_of(rank * tile, tile), tile), :] = corr[
            j, h, a * tile : (a + 1) * tile, :
        ]
        slot = slots_ref[0, p].astype(jnp.float32)
        buffer_ref[owner, pl.ds(CAP * tile + rank, 1), :] = jnp.full((1, LANES), slot, jnp.float32)


def remote(src, dst, send_sem, recv_sem, peer):
    return pltpu.make_async_remote_copy(
        src_ref=src, dst_ref=dst, send_sem=send_sem, recv_sem=recv_sem,
        device_id={"depth": peer}, device_id_type=pl.DeviceIdType.MESH,
    )


def meet(peers):
    barrier = pltpu.get_barrier_semaphore()
    for peer in peers:
        pl.semaphore_signal(
            barrier, inc=1, device_id={"depth": peer}, device_id_type=pl.DeviceIdType.MESH
        )
    pl.semaphore_wait(barrier, len(peers))


def gather_kernel(own_ref, library_ref, send_sem, recv_sem):
    me = lax.axis_index("depth")
    planes = library_ref.shape[0] // 4
    within = me % 4
    plane = me // 4
    core = me % 2
    pair = (me // 2) % 2

    def at(steps):
        return ((plane + steps + planes) % planes) * 4 + within

    beside = plane * 4 + (1 - pair) * 2 + core
    twin = me + 1 - 2 * core
    above, below = at(1), at(-1)
    meet([above, below, beside, twin])
    sent = []

    def send(block, peer):
        src = own_ref if block is me else library_ref.at[block]
        n = len(sent)
        copy = remote(src, library_ref.at[block], send_sem.at[n], recv_sem.at[block], peer)
        copy.start()
        sent.append(copy)

    def arrive(block):
        remote(own_ref, library_ref.at[block], send_sem.at[0], recv_sem.at[block], twin).wait_recv()

    up = planes // 2
    down = planes - 1 - up
    if up > 0:
        send(me, above)
    if down > 0:
        send(me, below)
    send(me, beside)
    send(me, twin)
    library_ref[me] = own_ref[...]
    order = [0]
    for step in range(1, up + 1):
        block = at(-step)
        order.append(-step)
        arrive(block)
        if step < up:
            send(block, above)
        send(block, beside)
        send(block, twin)
        if step <= down:
            block = at(step)
            order.append(step)
            arrive(block)
            if step < down:
                send(block, below)
            send(block, beside)
            send(block, twin)
    shift = (1 - 2 * pair) * 2
    for step in order:
        block = at(step) + shift
        arrive(block)
        send(block, twin)
    flip = 1 - 2 * core
    for step in order:
        arrive(at(step) + flip)
        arrive(at(step) + shift + flip)
    for copy in sent:
        copy.wait_send()


def volume_kernel(
    buffer_ref, volume_ref, across, landed, far, near, send_sem, far_sem, near_sem, cross_sem
):
    me = lax.axis_index("depth")
    peers = buffer_ref.shape[0]
    half = peers // 2
    tile = volume_ref.shape[1]
    step = 32
    side = me // half
    pos = me % half
    mirror = (me + half) % peers
    mates = [side * half + (pos + d) % half for d in range(1, half)]
    meet(mates + [mirror])
    far_copies, near_copies = [], []
    for d, mate in enumerate(mates, 1):
        copy = remote(
            buffer_ref.at[(mate + half) % peers], far.at[d], send_sem.at[d], far_sem.at[d], mate
        )
        copy.start()
        far_copies.append(copy)

    def clear(m, _):
        volume_ref[m] = jnp.zeros((tile, LANES), jnp.float32)
        across[m] = jnp.zeros((tile, LANES), jnp.float32)
        return 0

    lax.fori_loop(0, volume_ref.shape[0], clear, 0)

    def add_from(ref, block, total):
        for c in range(CAP):
            slot = ref[block, CAP * tile + c : CAP * tile + c + 1, :]
            slot = jnp.broadcast_to(slot, (8, LANES))
            slot = jnp.concatenate([slot] * (step // 8), axis=0)

            def body(i, _):
                r0 = pl.multiple_of(i * step, step)
                piece = ref[block, pl.ds(c * tile + r0, step), :]
                for m in range(IMG_SLOTS):
                    here = pl.ds(r0, step)
                    total[m, here, :] += jnp.where(slot == m, piece, 0.0)
                return 0

            lax.fori_loop(0, tile // step, body, 0)

    add_from(buffer_ref, mirror, across)
    for d, copy in enumerate(far_copies, 1):
        copy.wait_recv()
        add_from(far, d, across)
    add_from(buffer_ref, me, volume_ref)
    cross = remote(across, landed, send_sem.at[0], cross_sem, mirror)
    cross.start()
    for d, mate in enumerate(mates, 1):
        copy = remote(
            buffer_ref.at[mate], near.at[d], send_sem.at[half + d], near_sem.at[d], mate
        )
        copy.start()
        near_copies.append(copy)
    for d, copy in enumerate(near_copies, 1):
        copy.wait_recv()
        add_from(near, d, volume_ref)
    cross.wait_recv()

    def join(m, _):
        volume_ref[m] = volume_ref[m] + landed[m]
        return 0

    lax.fori_loop(0, volume_ref.shape[0], join, 0)
    for copy in far_copies + near_copies + [cross]:
        copy.wait_send()


def local(fields, vel_tiles, tile_ids, orders, term_weights, phase_rates, owners, image_slots):
    rows, columns = fields.shape[3:]
    tile = vel_tiles.shape[1]
    steps = tile_ids.shape[1]
    degrees = phase_rates.shape[0]
    halves = columns // LANES
    peers = lax.axis_size("depth")
    f32 = jnp.float32

    def shape(*dims):
        return jax.ShapeDtypeStruct(dims, f32)

    cost = pl.CostEstimate(flops=40_000_000, bytes_accessed=14_000_000, transcendentals=0)
    padded = [VMEM((2, halves, rows + 2 * HALO, LANES), f32)] * 3 + [
        VMEM((steps, degrees, 2, halves, rows, LANES), f32),
        pltpu.SemaphoreType.DMA((steps,)),
    ]

    library = pl.pallas_call(
        gather_kernel,
        out_shape=shape(peers, *vel_tiles.shape),
        in_specs=specs(VMEM),
        out_specs=specs(VMEM)[0],
        scratch_shapes=[pltpu.SemaphoreType.DMA((peers,)), pltpu.SemaphoreType.DMA((peers,))],
        compiler_params=pltpu.CompilerParams(collective_id=0, has_side_effects=True),
        name="gather",
    )(vel_tiles).reshape(peers * vel_tiles.shape[0], tile, tile)
    table = pl.pallas_call(
        table_kernel,
        out_shape=shape(steps, degrees, 2, halves, rows, LANES),
        in_specs=specs(SMEM, SMEM, SMEM, SMEM, VMEM),
        out_specs=specs(VMEM)[0],
        name="table",
    )(tile_ids, orders, term_weights, phase_rates, library)

    def half_of(which):
        return pl.BlockSpec(
            (None, None, 2, rows, columns), lambda i: (0, which, 0, 0, 0), memory_space=VMEM
        )

    def source_call(state, spec):
        return pl.pallas_call(
            source_kernel,
            grid=(1,),
            out_shape=(shape(max(steps - 1, 1), 2, rows, columns), shape(2, rows, columns)),
            in_specs=specs(pl.ANY) + [spec],
            out_specs=specs(VMEM, VMEM),
            scratch_shapes=padded,
            cost_estimate=cost,
            name="source_step",
        )(table, state)

    early, end = source_call(fields, half_of(0))
    source = from_behind(end, "depth", 1)
    receiver, correlation = pl.pallas_call(
        receiver_kernel,
        grid=(1,),
        out_shape=(shape(2, rows, columns), shape(steps, halves, rows, LANES)),
        in_specs=specs(pl.ANY) + [half_of(1)] + specs(VMEM, VMEM),
        out_specs=specs(VMEM, VMEM),
        scratch_shapes=padded,
        cost_estimate=cost,
        name="receiver_step",
    )(table, fields, early, end)
    receiver = from_behind(receiver, "depth", 1)
    early, end = source_call(source, specs(VMEM)[0])
    block_rows = CAP * tile + HALO
    wave, buffer = pl.pallas_call(
        final_kernel,
        out_shape=(shape(1, 2, 2, rows, columns), shape(peers, block_rows, LANES)),
        in_specs=specs(SMEM, SMEM, pl.ANY, VMEM, VMEM, VMEM, VMEM),
        out_specs=specs(VMEM, VMEM),
        scratch_shapes=[VMEM((steps, halves, rows, LANES), f32)] + padded,
        cost_estimate=cost,
        name="final_step",
    )(owners, image_slots, table, receiver, early, end, correlation)
    volume = pl.pallas_call(
        volume_kernel,
        out_shape=shape(IMG_SLOTS, tile, LANES),
        in_specs=specs(VMEM),
        out_specs=specs(VMEM)[0],
        scratch_shapes=[
            VMEM((IMG_SLOTS, tile, LANES), f32),
            VMEM((IMG_SLOTS, tile, LANES), f32),
            VMEM((peers // 2, block_rows, LANES), f32),
            VMEM((peers // 2, block_rows, LANES), f32),
            pltpu.SemaphoreType.DMA((peers,)),
            pltpu.SemaphoreType.DMA((peers // 2,)),
            pltpu.SemaphoreType.DMA((peers // 2,)),
            pltpu.SemaphoreType.DMA,
        ],
        compiler_params=pltpu.CompilerParams(collective_id=1, has_side_effects=True),
        name="volume",
    )(buffer)
    return volume, wave


def solution(mesh):
    whole = P(("groups", "depth"))
    placed = (whole, whole, whole, whole, P(), P(), whole, whole)
    return jax.shard_map(
        local, mesh=mesh, in_specs=placed, out_specs=(whole, whole), check_vma=False
    )
```

```python
import jax
import jax.numpy as jnp
from jax import lax
from jax.experimental import pallas as pl
from jax.experimental.pallas import tpu as pltpu
from jax.sharding import PartitionSpec as P

TICKS = 2
CAP = 2
IMG_SLOTS = 8
LANES = 128
HALO = 8
ROWS = 32
VMEM = pltpu.VMEM
SMEM = pltpu.SMEM


def specs(*spaces):
    return [pl.BlockSpec(memory_space=space) for space in spaces]


def from_behind(shard, axis, by):
    peers = lax.axis_size(axis)
    pairs = [(i, i + by) for i in range(peers) if 0 <= i + by < peers]
    return lax.ppermute(shard, axis, pairs)


def sincos(angle):
    turns = jnp.floor(angle * 0.6366197723675814 + 0.5)
    quarter = turns.astype(jnp.int32)
    r = angle - turns * 1.5703125
    r = r - turns * 4.838267948966192e-4
    r2 = r * r
    s = r + r * r2 * (-1.6666654611e-1 + r2 * (8.3321608736e-3 - r2 * 1.9515295891e-4))
    c = 1.0 - 0.5 * r2 + r2 * r2 * (
        4.166664568298827e-2 + r2 * (-1.388731625493765e-3 + r2 * 2.443315711809948e-5)
    )
    odd = (quarter & 1) == 1
    sin_out = jnp.where(odd, c, s)
    cos_out = jnp.where(odd, s, c)
    sin_out = jnp.where((quarter & 2) == 2, -sin_out, sin_out)
    cos_out = jnp.where(((quarter + 1) & 2) == 2, -cos_out, cos_out)
    return sin_out, cos_out


def table_kernel(ids_ref, orders_ref, term_ref, rates_ref, library_ref, table_ref):
    _, steps, tiles_x, tiles_y = ids_ref.shape
    degrees = rates_ref.shape[0]
    tile = library_ref.shape[1]
    zeroth = 1.0 - sum(term_ref[k] for k in range(degrees - 1))
    for j in range(steps):
        order = orders_ref[0, j]
        weights = [zeroth] + [
            jnp.where(order >= k, term_ref[k - 1], 0.0) for k in range(1, degrees)
        ]
        for b in range(tiles_y):
            for a in range(tiles_x):
                source = ids_ref[0, j, a, b]

                def body(i, _):
                    r0 = pl.multiple_of(i * ROWS, ROWS)
                    slow = library_ref[source, pl.ds(r0, ROWS), :]
                    for k in range(degrees):
                        sin_now, cos_now = sincos(rates_ref[k] * slow)
                        rows = pl.ds(a * tile + r0, ROWS)
                        table_ref[j, k, 0, b, rows, :] = weights[k] * cos_now
                        table_ref[j, k, 1, b, rows, :] = weights[k] * sin_now
                    return 0

                lax.fori_loop(0, tile // ROWS, body, 0)


def smooth(ref, f, halves, r0, lane):
    centre, down = [], []
    for h in range(halves):
        c = ref[f, h, pl.ds(r0 + HALO, ROWS), :]
        u = ref[f, h, pl.ds(r0 + HALO - 1, ROWS), :]
        d = ref[f, h, pl.ds(r0 + HALO + 1, ROWS), :]
        centre.append(c)
        down.append((u + d) + (c + c))
    right = [pltpu.roll(v, 1, 1) for v in down]
    left = [pltpu.roll(v, LANES - 1, 1) for v in down]
    out = []
    for h in range(halves):
        before = jnp.where(lane == 0, right[h - 1] if h else 0.0, right[h])
        after = jnp.where(lane == LANES - 1, left[h + 1] if h + 1 < halves else 0.0, left[h])
        out.append((before + after) + (down[h] + down[h]))
    return out, centre


def clear_halos(refs, halves, rows):
    zero = jnp.zeros((HALO, LANES), jnp.float32)
    for ref in refs:
        for f in range(2):
            for h in range(halves):
                ref[f, h, 0:HALO, :] = zero
                ref[f, h, rows + HALO : rows + 2 * HALO, :] = zero


def load_state(state_ref, p0, halves, rows):
    def body(i, _):
        r0 = pl.multiple_of(i * ROWS, ROWS)
        for f in range(2):
            for h in range(halves):
                p0[f, h, pl.ds(r0 + HALO, ROWS), :] = state_ref[
                    f, pl.ds(r0, ROWS), h * LANES : (h + 1) * LANES
                ]
        return 0

    lax.fori_loop(0, rows // ROWS, body, 0)


def fetch(table_ref, table, sems):
    copies = [
        pltpu.make_async_copy(table_ref.at[j], table.at[j], sems.at[j])
        for j in range(table_ref.shape[0])
    ]
    for copy in copies:
        copy.start()
    return copies


def depth_step(table_ref, copy, j, sign, p0, p1, p2, halves, rows, emit):
    lane = lax.broadcasted_iota(jnp.int32, (ROWS, LANES), 1)
    chunks = rows // ROWS

    def first(i, _):
        r0 = pl.multiple_of(i * ROWS, ROWS)
        for f in range(2):
            soft, centre = smooth(p0, f, halves, r0, lane)
            for h in range(halves):
                p1[f, h, pl.ds(r0 + HALO, ROWS), :] = 0.125 * soft[h] - centre[h]
        return 0

    def second(i, _):
        r0 = pl.multiple_of(i * ROWS, ROWS)
        for f in range(2):
            soft, centre = smooth(p1, f, halves, r0, lane)
            for h in range(halves):
                here = pl.ds(r0 + HALO, ROWS)
                p2[f, h, here, :] = 0.25 * soft[h] - 2.0 * centre[h] - p0[f, h, here, :]
        return 0

    def third(i, _):
        r0 = pl.multiple_of(i * ROWS, ROWS)
        here = pl.ds(r0 + HALO, ROWS)
        terms = []
        for f in range(2):
            soft, centre = smooth(p2, f, halves, r0, lane)
            terms.append((soft, centre))
        for h in range(halves):
            series = []
            for f in range(2):
                soft, centre = terms[f]
                t0 = p0[f, h, here, :]
                t1 = p1[f, h, here, :]
                series.append((t0, t1, centre[h], 0.25 * soft[h] - 2.0 * centre[h] - t1))
            real = imag = None
            for k in range(4):
                a = table_ref[j, k, 0, h, pl.ds(r0, ROWS), :]
                b = table_ref[j, k, 1, h, pl.ds(r0, ROWS), :]
                re, im = series[0][k], series[1][k]
                if sign > 0:
                    new_real, new_imag = a * re - b * im, a * im + b * re
                else:
                    new_real, new_imag = a * re + b * im, a * im - b * re
                real = new_real if real is None else real + new_real
                imag = new_imag if imag is None else imag + new_imag
            p0[0, h, here, :] = real
            p0[1, h, here, :] = imag
            emit(j, h, r0, real, imag)
        return 0

    lax.fori_loop(0, chunks, first, 0, unroll=2)
    lax.fori_loop(0, chunks, second, 0, unroll=2)
    copy.wait()
    lax.fori_loop(0, chunks, third, 0, unroll=2)


def source_kernel(table_ref, state_ref, out_ref, end_ref, p0, p1, p2, table, sems):
    copies = fetch(table_ref, table, sems)
    halves, rows = table_ref.shape[3], table_ref.shape[4]
    clear_halos((p0, p1, p2), halves, rows)
    load_state(state_ref, p0, halves, rows)

    def emit(j, h, r0, real, imag):
        columns = slice(h * LANES, (h + 1) * LANES)
        here = pl.ds(r0, ROWS)
        target = end_ref if j == table_ref.shape[0] - 1 else out_ref.at[j]
        target[0, here, columns] = real
        target[1, here, columns] = imag

    for j in range(table_ref.shape[0]):
        depth_step(table, copies[j], j, 1.0, p0, p1, p2, halves, rows, emit)


def receiver_kernel(table_ref, state_ref, steps_ref, end_ref, out_ref, corr_ref, p0, p1, p2, table, sems):
    copies = fetch(table_ref, table, sems)
    halves, rows = table_ref.shape[3], table_ref.shape[4]
    clear_halos((p0, p1, p2), halves, rows)
    load_state(state_ref, p0, halves, rows)
    last = table_ref.shape[0] - 1

    def emit(j, h, r0, real, imag):
        columns = slice(h * LANES, (h + 1) * LANES)
        here = pl.ds(r0, ROWS)
        if j == last:
            out_ref[0, here, columns] = real
            out_ref[1, here, columns] = imag
        source = end_ref if j == last else steps_ref.at[j]
        corr_ref[j, h, here, :] = source[0, here, columns] * real + source[1, here, columns] * imag

    for j in range(last + 1):
        depth_step(table, copies[j], j, -1.0, p0, p1, p2, halves, rows, emit)


def final_kernel(
    owners_ref, slots_ref, table_ref, state_ref, steps_ref, end_ref, before_ref,
    wave_ref, buffer_ref, corr, p0, p1, p2, table, sems,
):
    copies = fetch(table_ref, table, sems)
    halves, rows = table_ref.shape[3], table_ref.shape[4]
    clear_halos((p0, p1, p2), halves, rows)
    load_state(state_ref, p0, halves, rows)
    steps = table_ref.shape[0]
    last = steps - 1
    tile = LANES
    tiles_x = rows // tile

    def emit(j, h, r0, real, imag):
        columns = slice(h * LANES, (h + 1) * LANES)
        here = pl.ds(r0, ROWS)
        source = end_ref if j == last else steps_ref.at[j]
        src_real = source[0, here, columns]
        src_imag = source[1, here, columns]
        if j == last:
            wave_ref[0, 0, 0, here, columns] = src_real
            wave_ref[0, 0, 1, here, columns] = src_imag
            wave_ref[0, 1, 0, here, columns] = real
            wave_ref[0, 1, 1, here, columns] = imag
        corr[j, h, here, :] = before_ref[j, h, here, :] + (src_real * real + src_imag * imag)

    for j in range(steps):
        depth_step(table, copies[j], j, -1.0, p0, p1, p2, halves, rows, emit)

    peers = buffer_ref.shape[0]

    def clear(o, _):
        buffer_ref[o] = jnp.zeros(buffer_ref.shape[1:], jnp.float32)
        buffer_ref[o, CAP * tile : CAP * tile + CAP, :] = jnp.full((CAP, LANES), -1.0, jnp.float32)
        return 0

    lax.fori_loop(0, peers, clear, 0)
    pieces = owners_ref.shape[1]

    for p in range(pieces):
        owner = owners_ref[0, p]
        rank = 0
        for q in range(p):
            rank = rank + jnp.where(owners_ref[0, q] == owner, 1, 0)
        j, rest = divmod(p, tiles_x * halves)
        a, h = divmod(rest, halves)
        buffer_ref[owner, pl.ds(pl.multiple_of(rank * tile, tile), tile), :] = corr[
            j, h, a * tile : (a + 1) * tile, :
        ]
        slot = slots_ref[0, p].astype(jnp.float32)
        buffer_ref[owner, pl.ds(CAP * tile + rank, 1), :] = jnp.full((1, LANES), slot, jnp.float32)


def remote(src, dst, send_sem, recv_sem, peer):
    return pltpu.make_async_remote_copy(
        src_ref=src, dst_ref=dst, send_sem=send_sem, recv_sem=recv_sem,
        device_id={"depth": peer}, device_id_type=pl.DeviceIdType.MESH,
    )


def meet(peers):
    barrier = pltpu.get_barrier_semaphore()
    for peer in peers:
        pl.semaphore_signal(
            barrier, inc=1, device_id={"depth": peer}, device_id_type=pl.DeviceIdType.MESH
        )
    pl.semaphore_wait(barrier, len(peers))


def gather_kernel(own_ref, library_ref, send_sem, recv_sem):
    me = lax.axis_index("depth")
    planes = library_ref.shape[0] // 4
    within = me % 4
    plane = me // 4
    core = me % 2
    pair = (me // 2) % 2

    def at(steps):
        return ((plane + steps + planes) % planes) * 4 + within

    beside = plane * 4 + (1 - pair) * 2 + core
    twin = me + 1 - 2 * core
    above, below = at(1), at(-1)
    meet([above, below, beside, twin])
    sent = []

    def send(block, peer):
        src = own_ref if block is me else library_ref.at[block]
        n = len(sent)
        copy = remote(src, library_ref.at[block], send_sem.at[n], recv_sem.at[block], peer)
        copy.start()
        sent.append(copy)

    def arrive(block):
        remote(own_ref, library_ref.at[block], send_sem.at[0], recv_sem.at[block], twin).wait_recv()

    up = planes // 2
    down = planes - 1 - up
    if up > 0:
        send(me, above)
    if down > 0:
        send(me, below)
    send(me, beside)
    send(me, twin)
    library_ref[me] = own_ref[...]
    order = [0]
    for step in range(1, up + 1):
        block = at(-step)
        order.append(-step)
        arrive(block)
        if step < up:
            send(block, above)
        send(block, beside)
        send(block, twin)
        if step <= down:
            block = at(step)
            order.append(step)
            arrive(block)
            if step < down:
                send(block, below)
            send(block, beside)
            send(block, twin)
    shift = (1 - 2 * pair) * 2
    for step in order:
        block = at(step) + shift
        arrive(block)
        send(block, twin)
    flip = 1 - 2 * core
    for step in order:
        arrive(at(step) + flip)
        arrive(at(step) + shift + flip)
    for copy in sent:
        copy.wait_send()


def volume_kernel(
    buffer_ref, volume_ref, across, landed, far, near, send_sem, far_sem, near_sem, cross_sem
):
    me = lax.axis_index("depth")
    peers = buffer_ref.shape[0]
    half = peers // 2
    tile = volume_ref.shape[1]
    step = 32
    side = me // half
    pos = me % half
    mirror = (me + half) % peers
    mates = [side * half + (pos + d) % half for d in range(1, half)]
    meet(mates + [mirror])
    far_copies, near_copies = [], []
    for d, mate in enumerate(mates, 1):
        copy = remote(
            buffer_ref.at[(mate + half) % peers], far.at[d], send_sem.at[d], far_sem.at[d], mate
        )
        copy.start()
        far_copies.append(copy)

    def clear(m, _):
        volume_ref[m] = jnp.zeros((tile, LANES), jnp.float32)
        across[m] = jnp.zeros((tile, LANES), jnp.float32)
        return 0

    lax.fori_loop(0, volume_ref.shape[0], clear, 0)

    def add_from(ref, block, total):
        for c in range(CAP):
            slot = ref[block, CAP * tile + c : CAP * tile + c + 1, :]
            slot = jnp.broadcast_to(slot, (8, LANES))
            slot = jnp.concatenate([slot] * (step // 8), axis=0)

            def body(i, _):
                r0 = pl.multiple_of(i * step, step)
                piece = ref[block, pl.ds(c * tile + r0, step), :]
                for m in range(IMG_SLOTS):
                    here = pl.ds(r0, step)
                    total[m, here, :] += jnp.where(slot == m, piece, 0.0)
                return 0

            lax.fori_loop(0, tile // step, body, 0)

    add_from(buffer_ref, mirror, across)
    for d, copy in enumerate(far_copies, 1):
        copy.wait_recv()
        add_from(far, d, across)
    add_from(buffer_ref, me, volume_ref)
    cross = remote(across, landed, send_sem.at[0], cross_sem, mirror)
    cross.start()
    for d, mate in enumerate(mates, 1):
        copy = remote(
            buffer_ref.at[mate], near.at[d], send_sem.at[half + d], near_sem.at[d], mate
        )
        copy.start()
        near_copies.append(copy)
    for d, copy in enumerate(near_copies, 1):
        copy.wait_recv()
        add_from(near, d, volume_ref)
    cross.wait_recv()

    def join(m, _):
        volume_ref[m] = volume_ref[m] + landed[m]
        return 0

    lax.fori_loop(0, volume_ref.shape[0], join, 0)
    for copy in far_copies + near_copies + [cross]:
        copy.wait_send()


def local(fields, vel_tiles, tile_ids, orders, term_weights, phase_rates, owners, image_slots):
    rows, columns = fields.shape[3:]
    tile = vel_tiles.shape[1]
    steps = tile_ids.shape[1]
    degrees = phase_rates.shape[0]
    halves = columns // LANES
    peers = lax.axis_size("depth")
    f32 = jnp.float32

    def shape(*dims):
        return jax.ShapeDtypeStruct(dims, f32)

    cost = pl.CostEstimate(flops=40_000_000, bytes_accessed=14_000_000, transcendentals=0)
    padded = [VMEM((2, halves, rows + 2 * HALO, LANES), f32)] * 3 + [
        VMEM((steps, degrees, 2, halves, rows, LANES), f32),
        pltpu.SemaphoreType.DMA((steps,)),
    ]

    library = pl.pallas_call(
        gather_kernel,
        out_shape=shape(peers, *vel_tiles.shape),
        in_specs=specs(VMEM),
        out_specs=specs(VMEM)[0],
        scratch_shapes=[pltpu.SemaphoreType.DMA((peers,)), pltpu.SemaphoreType.DMA((peers,))],
        compiler_params=pltpu.CompilerParams(collective_id=0, has_side_effects=True),
        name="gather",
    )(vel_tiles).reshape(peers * vel_tiles.shape[0], tile, tile)
    table = pl.pallas_call(
        table_kernel,
        out_shape=shape(steps, degrees, 2, halves, rows, LANES),
        in_specs=specs(SMEM, SMEM, SMEM, SMEM, VMEM),
        out_specs=specs(VMEM)[0],
        name="table",
    )(tile_ids, orders, term_weights, phase_rates, library)

    def half_of(which):
        return pl.BlockSpec(
            (None, None, 2, rows, columns), lambda i: (0, which, 0, 0, 0), memory_space=VMEM
        )

    def source_call(state, spec):
        return pl.pallas_call(
            source_kernel,
            grid=(1,),
            out_shape=(shape(max(steps - 1, 1), 2, rows, columns), shape(2, rows, columns)),
            in_specs=specs(pl.ANY) + [spec],
            out_specs=specs(VMEM, VMEM),
            scratch_shapes=padded,
            cost_estimate=cost,
            name="source_step",
        )(table, state)

    early, end = source_call(fields, half_of(0))
    source = from_behind(end, "depth", 1)
    receiver, correlation = pl.pallas_call(
        receiver_kernel,
        grid=(1,),
        out_shape=(shape(2, rows, columns), shape(steps, halves, rows, LANES)),
        in_specs=specs(pl.ANY) + [half_of(1)] + specs(VMEM, VMEM),
        out_specs=specs(VMEM, VMEM),
        scratch_shapes=padded,
        cost_estimate=cost,
        name="receiver_step",
    )(table, fields, early, end)
    receiver = from_behind(receiver, "depth", 1)
    early, end = source_call(source, specs(VMEM)[0])
    block_rows = CAP * tile + HALO
    wave, buffer = pl.pallas_call(
        final_kernel,
        out_shape=(shape(1, 2, 2, rows, columns), shape(peers, block_rows, LANES)),
        in_specs=specs(SMEM, SMEM, pl.ANY, VMEM, VMEM, VMEM, VMEM),
        out_specs=specs(VMEM, VMEM),
        scratch_shapes=[VMEM((steps, halves, rows, LANES), f32)] + padded,
        cost_estimate=cost,
        name="final_step",
    )(owners, image_slots, table, receiver, early, end, correlation)
    volume = pl.pallas_call(
        volume_kernel,
        out_shape=shape(IMG_SLOTS, tile, LANES),
        in_specs=specs(VMEM),
        out_specs=specs(VMEM)[0],
        scratch_shapes=[
            VMEM((IMG_SLOTS, tile, LANES), f32),
            VMEM((IMG_SLOTS, tile, LANES), f32),
            VMEM((peers // 2, block_rows, LANES), f32),
            VMEM((peers // 2, block_rows, LANES), f32),
            pltpu.SemaphoreType.DMA((peers,)),
            pltpu.SemaphoreType.DMA((peers // 2,)),
            pltpu.SemaphoreType.DMA((peers // 2,)),
            pltpu.SemaphoreType.DMA,
        ],
        compiler_params=pltpu.CompilerParams(collective_id=1, has_side_effects=True),
        name="volume",
    )(buffer)
    return volume, wave


def solution(mesh):
    whole = P(("groups", "depth"))
    placed = (whole, whole, whole, whole, P(), P(), whole, whole)
    return jax.shard_map(
        local, mesh=mesh, in_specs=placed, out_specs=(whole, whole), check_vma=False
    )
```
